512 devices in a mesh: row: 8 (over x, core), col: 64 (over z, y).
Axes of the slice: x: 4, y: 8, z: 8, core: 2. Of those that a mesh axis runs over, the one named last changes fastest.
Arguments:
- density: float32 [32768, 1216], P(('row', 'col')), as said below
- pattern: int32 [512, 19], P(('row', 'col')), may hold values from 0 to 1, as said below
Outputs:
- purified: float32 [32768, 1216], P(('row', 'col'))
The draws below stay inside these ranges and needn't reach their ends.
Inputs may be any that keep to these rules, and one draw needn't show every extreme that they name: pattern[i, s] equals pattern[i + s - 9, 18 - s]; pattern[i, 9] is 1; pattern[i, s] is 0 where i + s - 9 lies outside 0 to 511. `density`: block (i, s) is zero where pattern is 0.
All inputs are finite; a program needn't handle non-finite values.
Results may differ from the reference program's by a relative error of at most 0.007.
Values may be sent and summed in bfloat16 or wider, within the bound.
A program may use at most 64 MiB of HBM per device.

```python
import math
import jax
import jax.numpy as jnp

BLOCK = 64
HALF = 9
STEPS = 2
SLOTS = 19
NBLK = 512


def pattern_band(key):
    inner_key = jax.random.fold_in(key, 7)
    level_key, pick_key = jax.random.split(inner_key)
    levels = jax.random.randint(level_key, (NBLK,), 3, 9)
    pick_draw = jax.random.randint(pick_key, (NBLK, SLOTS), 0, 8)
    places = jnp.arange(NBLK)[:, None]
    offsets = jnp.arange(SLOTS)[None, :] - HALF
    partner = places + offsets
    inside = (partner >= 0) & (partner < NBLK)
    partner_safe = jnp.clip(partner, 0, NBLK - 1)
    lower_index = jnp.minimum(places, partner_safe)
    distance = jnp.abs(offsets)
    chosen = pick_draw[lower_index, HALF + distance]
    bounds = jnp.minimum(levels[places], levels[partner_safe])
    kept_flags = jnp.where(distance == 0, 1, (chosen < bounds).astype(jnp.int32))
    return jnp.where(inside, kept_flags, 0).astype(jnp.int32)


def draw_pattern(key, part):
    return pattern_band(key)


def draw_density(key, part):
    band_table = pattern_band(key)
    inner_key = jax.random.fold_in(key, 13)
    noise_key, diag_key = jax.random.split(inner_key)
    spread = 0.4 / math.sqrt(SLOTS * BLOCK)
    noise_draw = jax.random.normal(noise_key, (NBLK, SLOTS, BLOCK, BLOCK), jnp.float32)
    diagonal = jax.random.uniform(diag_key, (NBLK, BLOCK), jnp.float32, 0.2, 0.8)
    padded = jnp.pad(noise_draw, ((HALF, HALF), (0, 0), (0, 0), (0, 0)))
    mirrored = jnp.stack([jnp.swapaxes(padded[offset:offset + NBLK, 2 * HALF - offset], 1, 2) for offset in range(SLOTS)], axis=1)
    mixed = (noise_draw + mirrored) * (spread * 0.70710678)
    masked = band_table.astype(jnp.float32)[:, :, None, None] * mixed
    slot_here = jnp.arange(SLOTS)[:, None, None] == HALF
    same_entry = jnp.arange(BLOCK)[:, None] == jnp.arange(BLOCK)[None, :]
    on_diag = slot_here & same_entry[None]
    values = jnp.where(on_diag[None], diagonal[:, None, :, None], masked)
    return jnp.transpose(values, (0, 2, 1, 3)).reshape(NBLK * BLOCK, SLOTS * BLOCK).astype(jnp.float32)


def setup_inputs(seed: int = 0) -> dict:
    key_of = jax.random.split(jax.random.key(seed), 3)
    density = draw_density(jax.random.fold_in(key_of[2], 71), 0)
    pattern = draw_pattern(jax.random.fold_in(key_of[2], 71), 0)
    return {"density": density, "pattern": pattern}


def apply_mask(values, pattern_rows):
    rows_total, full_width = values.shape
    blocks = rows_total // BLOCK
    shaped = values.reshape(blocks, BLOCK, SLOTS, BLOCK)
    factor = pattern_rows.astype(values.dtype)[:, None, :, None]
    return (shaped * factor).reshape(rows_total, full_width)


def band_product(left_rows, far_rows):
    rows_total = left_rows.shape[0]
    blocks = rows_total // BLOCK
    outputs = []
    for out_slot in range(SLOTS):
        first_slot = max(0, out_slot - HALF)
        last_slot = min(2 * HALF, out_slot + HALF)
        slot_span = last_slot - first_slot + 1
        shift_start = first_slot - out_slot + HALF
        left_part = left_rows[:, first_slot * BLOCK:(last_slot + 1) * BLOCK].astype(jnp.float32).reshape(blocks, BLOCK, slot_span * BLOCK)
        right_part = far_rows[out_slot * BLOCK:out_slot * BLOCK + rows_total, shift_start * BLOCK:(shift_start + slot_span) * BLOCK].astype(jnp.float32).reshape(blocks, BLOCK, slot_span * BLOCK)
        outputs.append(jnp.einsum("iax,ibx->iab", left_part, right_part))
    return jnp.stack(outputs, axis=2).reshape(rows_total, SLOTS * BLOCK)


def reference(density, pattern):
    current = density
    for iteration in range(STEPS):
        lowered = current.astype(jnp.bfloat16)
        far_rows = jnp.pad(lowered, ((HALF * BLOCK, HALF * BLOCK), (0, 0)))
        square = apply_mask(band_product(lowered, far_rows), pattern)
        square_low = square.astype(jnp.bfloat16)
        cube_term = band_product(square_low, far_rows)
        current = apply_mask(3.0 * square - 2.0 * cube_term, pattern)
    return current
```

```python
import functools

import jax
import jax.numpy as jnp
from jax import lax
from jax.experimental import pallas as pl
from jax.experimental.pallas import tpu as pltpu
from jax.sharding import PartitionSpec as P

STEPS = 2
BLOCK = 64
HALF = 9
SLOTS = 2 * HALF + 1
LANES = 128
TILES = 10
WIDTH = TILES * LANES
FULL = SLOTS * BLOCK
STORED = 13
LINE = 8
EVENS = 9 * BLOCK
ODDS = 10 * BLOCK
MESH = pl.DeviceIdType.MESH


def offset_of(d):
    return (d + 1) // 2


def rows_of(step, d):
    order = (d + HALF - 1) // 2 if d % 2 == 0 else HALF + (d + HALF) // 2
    return pl.ds(step * FULL + order * BLOCK, BLOCK)


def needed_tiles(d):
    if d > 0:
        return 0, (2 * HALF - d) // 2
    return (-d) // 2, TILES - 1


ROUTES = []
for near in (1, 2, 3, 4):
    ROUTES.append((-near, 1, 1 - near))
    ROUTES.append((near, -1, near - 1))
for far in (5, 6, 7, 8, 9):
    ROUTES.append((-far, LINE, LINE - far))
    ROUTES.append((far, -LINE, far - LINE))


def tiles_sent(d):
    if abs(d) <= 3:
        return 0, TILES - 1
    return needed_tiles(d)


def kernel(total, columns, dens_ref, pat_ref, out_ref, band, shifted, squares, low, send_sem, recv_sem):
    me = lax.axis_index("row") * columns + lax.axis_index("col")

    def place(index):
        return (index // columns, lax.rem(index, columns))

    def copy(step, d, delta, source):
        first, last = tiles_sent(d)
        there = me + delta
        span = (last - first + 1) * LANES
        return pltpu.make_async_remote_copy(
            src_ref=band.at[rows_of(step, source), pl.ds((1 + first + offset_of(source)) * LANES, span)],
            dst_ref=band.at[rows_of(step, d), pl.ds((1 + first + offset_of(d)) * LANES, span)],
            send_sem=send_sem.at[step, d + HALF],
            recv_sem=recv_sem.at[step, d + HALF],
            device_id=place(there),
            device_id_type=MESH,
        )

    def inside(index):
        return (index >= 0) & (index < total)


    def edge_target(d):
        there = me - d
        if d < 0:
            return (there < LINE) & (there < total)
        return (there >= total - LINE) & (there >= 0)

    def edge_source(d):
        if d < 0:
            return (me < LINE) & (me + d >= 0)
        return (me >= total - LINE) & (me + d < total)

    EDGES = [d for far in (5, 6, 7) for d in (-far, far)]

    for step in range(STEPS):
        for d in range(-HALF, HALF + 1):
            if d == 0:
                continue
            off = offset_of(d)
            if d > 0:
                band[rows_of(step, d), LANES:(1 + off) * LANES] = jnp.zeros((BLOCK, off * LANES), jnp.bfloat16)
            elif off < 0:
                band[rows_of(step, d), (1 + TILES + off) * LANES:(1 + TILES) * LANES] = jnp.zeros((BLOCK, -off * LANES), jnp.bfloat16)

            @pl.when(jnp.logical_not(inside(me + d)))
            def _():
                band[rows_of(step, d), LANES:(1 + TILES) * LANES] = jnp.zeros((BLOCK, WIDTH), jnp.bfloat16)

    barrier = pltpu.get_barrier_semaphore()
    count = jnp.int32(0)
    for delta in (-LINE, -1, 1, LINE):
        there = me + delta

        @pl.when(inside(there))
        def _():
            pl.semaphore_signal(barrier, inc=1, device_id=place(there), device_id_type=MESH)

        count += inside(there).astype(jnp.int32)
    for d in EDGES:
        @pl.when(edge_target(d))
        def _():
            pl.semaphore_signal(barrier, inc=1, device_id=place(me - d), device_id_type=MESH)

        @pl.when(edge_source(d))
        def _():
            pl.semaphore_signal(barrier, inc=1, device_id=place(me + d), device_id_type=MESH)

        count += edge_target(d).astype(jnp.int32) + edge_source(d).astype(jnp.int32)
    pl.semaphore_wait(barrier, count)

    low[0:BLOCK, :] = jnp.zeros((BLOCK, BLOCK), jnp.bfloat16)
    low[(SLOTS + 1) * BLOCK:(SLOTS + 2) * BLOCK, :] = jnp.zeros((BLOCK, BLOCK), jnp.bfloat16)
    squares[(SLOTS + 1) * BLOCK:(SLOTS + 2) * BLOCK, :] = jnp.zeros((BLOCK, BLOCK), jnp.float32)
    squares[0:BLOCK, :] = jnp.zeros((BLOCK, BLOCK), jnp.float32)

    def forward(step, source):
        for d, delta, from_slot in ROUTES:
            if from_slot == source:
                @pl.when(inside(me + delta) & inside(me + source))
                def _():
                    copy(step, d, delta, source).start()

    def has_route(d):
        delta = [entry[1] for entry in ROUTES if entry[0] == d][0]
        return inside(me + d) & inside(me - delta)

    def wait_for(step, d):
        present = has_route(d)
        if d in EDGES:
            present = present | edge_source(d)

        @pl.when(present)
        def _():
            copy(step, d, 0, 0).wait_recv()

    for step in range(STEPS):
        own = rows_of(step, 0)
        if step == 0:
            current = dens_ref[...]
            band[own, LANES:LANES + FULL] = current.astype(jnp.bfloat16)
            band[own, LANES + FULL:LANES + WIDTH] = jnp.zeros((BLOCK, WIDTH - FULL), jnp.bfloat16)
        else:
            for tile in range(TILES):
                part = squares[(1 + 2 * tile) * BLOCK:(3 + 2 * tile) * BLOCK, :]
                band[own, (1 + tile) * LANES:(2 + tile) * LANES] = part.T.astype(jnp.bfloat16)
        forward(step, 0)
        for d in EDGES:
            @pl.when(edge_target(d))
            def _():
                copy(step, d, -d, 0).start()
        if step == 0:
            padded = jnp.concatenate([jnp.zeros((BLOCK, BLOCK), jnp.float32), current], axis=1)
            shifted[...] = padded.astype(jnp.bfloat16)
        else:
            for tile in range(TILES):
                part = squares[2 * tile * BLOCK:(2 + 2 * tile) * BLOCK, :]
                shifted[:, tile * LANES:(1 + tile) * LANES] = part.T.astype(jnp.bfloat16)
        for near in (1, 2, 3):
            for d in (-near, near):
                wait_for(step, d)
                forward(step, d)
        for near in (4, 5, 6, 7, 8, 9):
            for d in (-near, near):
                wait_for(step, d)
        window = slice(LANES, LANES + WIDTH)
        even_rows = band[pl.ds(step * FULL, EVENS), window]
        odd_rows = band[pl.ds(step * FULL + EVENS, ODDS), window]
        across = (((1,), (1,)), ((), ()))
        even_square = lax.dot_general(even_rows, band[own, window], across, preferred_element_type=jnp.float32)
        odd_square = lax.dot_general(odd_rows, shifted[...], across, preferred_element_type=jnp.float32)
        for slot in range(SLOTS):
            order = (slot - 1) // 2 if slot % 2 else slot // 2
            source = even_square if slot % 2 else odd_square
            kept = pat_ref[0, slot].astype(jnp.float32)
            part = source[order * BLOCK:(order + 1) * BLOCK, :] * kept
            squares[(1 + slot) * BLOCK:(2 + slot) * BLOCK, :] = part
            low[(1 + slot) * BLOCK:(2 + slot) * BLOCK, :] = part.astype(jnp.bfloat16)
        even_cube = jnp.dot(even_rows, low[BLOCK:BLOCK + WIDTH, :], preferred_element_type=jnp.float32)
        odd_cube = jnp.dot(odd_rows, low[0:WIDTH, :], preferred_element_type=jnp.float32)
        for slot in range(SLOTS):
            order = (slot - 1) // 2 if slot % 2 else slot // 2
            source = even_cube if slot % 2 else odd_cube
            kept = pat_ref[0, slot].astype(jnp.float32)
            part = squares[(1 + slot) * BLOCK:(2 + slot) * BLOCK, :]
            cube = source[order * BLOCK:(order + 1) * BLOCK, :]
            squares[(1 + slot) * BLOCK:(2 + slot) * BLOCK, :] = (3.0 * part - 2.0 * cube) * kept

    for tile in range(TILES):
        part = squares[(1 + 2 * tile) * BLOCK:(3 + 2 * tile) * BLOCK, :].T
        wide = min(LANES, FULL - tile * LANES)
        out_ref[:, tile * LANES:tile * LANES + wide] = part[:, :wide]

    for step in range(STEPS):
        for d, delta, source in ROUTES:
            @pl.when(inside(me + delta) & inside(me + source))
            def _():
                copy(step, d, delta, source).wait_send()
        for d in EDGES:
            @pl.when(edge_target(d))
            def _():
                copy(step, d, -d, 0).wait_send()


def solution(mesh):
    columns = mesh.shape["col"]
    total = mesh.shape["row"] * columns

    def local(density, pattern):
        return pl.pallas_call(
            functools.partial(kernel, total, columns),
            out_shape=jax.ShapeDtypeStruct((BLOCK, FULL), jnp.float32),
            in_specs=[
                pl.BlockSpec(memory_space=pltpu.VMEM),
                pl.BlockSpec(memory_space=pltpu.SMEM),
            ],
            out_specs=pl.BlockSpec(memory_space=pltpu.VMEM),
            scratch_shapes=[
                pltpu.VMEM((STEPS * FULL, STORED * LANES), jnp.bfloat16),
                pltpu.VMEM((BLOCK, WIDTH), jnp.bfloat16),
                pltpu.VMEM(((SLOTS + 2) * BLOCK, BLOCK), jnp.float32),
                pltpu.VMEM(((SLOTS + 2) * BLOCK, BLOCK), jnp.bfloat16),
                pltpu.SemaphoreType.DMA((STEPS, SLOTS)),
                pltpu.SemaphoreType.DMA((STEPS, SLOTS)),
            ],
            compiler_params=pltpu.CompilerParams(
                collective_id=0, has_side_effects=True, vmem_limit_bytes=40 << 20
            ),
        )(density, pattern)

    placed = (P(("row", "col"), None), P(("row", "col"), None))
    return jax.shard_map(
        local, mesh=mesh, in_specs=placed, out_specs=P(("row", "col"), None), check_vma=False
    )
```

```python
import functools

import jax
import jax.numpy as jnp
from jax import lax
from jax.experimental import pallas as pl
from jax.experimental.pallas import tpu as pltpu
from jax.sharding import PartitionSpec as P

STEPS = 2
BLOCK = 64
HALF = 9
SLOTS = 2 * HALF + 1
LANES = 128
TILES = 10
WIDTH = TILES * LANES
FULL = SLOTS * BLOCK
LINE = 8
EVENS = 9 * BLOCK
ODDS = 10 * BLOCK
MARGIN = 4
STORED = TILES + 9
CUT = 5
PARTS = ((0, CUT - 1), (CUT, TILES - 1))
MESH = pl.DeviceIdType.MESH

ROUTES = (
    ((8, 1, 1, 0), (-8, 0, -1, 0), (7, 1, 0, 7), (1, 0, 0, 1), (8, 0, 1, 0), (-8, 1, -1, 0), (7, 0, 0, 7),
     (1, 1, 0, 1), (-7, 0, 0, 1), (-9, 0, -1, 7), (-1, 1, -1, 0), (2, 0, 0, 1), (6, 0, 0, 7), (9, 0, 1, 0),
     (6, 1, 0, 7), (-1, 0, -1, 0), (-7, 1, 0, 1), (2, 1, 0, 1), (5, 1, 0, 7), (-9, 1, -1, 0), (-6, 0, -1, 0),
     (-2, 0, -1, 0), (4, 1, 0, 6), (-2, 1, 0, 7), (-6, 1, -1, 0), (4, 0, 0, 1), (5, 0, 0, 7), (-5, 0, 0, 1),
     (-3, 1, -1, 0), (3, 0, 0, 7), (-4, 0, 0, 1), (-4, 1, -1, 0), (3, 1, 0, 7), (-5, 1, 0, 1), (-3, 0, -1, 0)),
    ((-8, 0, -1, 1), (1, 0, 0, 2), (-1, 0, 0, 0), (8, 0, 1, 1), (8, 1, 1, 1), (-8, 1, -1, 1), (1, 1, 0, 2),
     (-1, 1, 0, 0), (7, 1, 0, 0), (-7, 0, 0, 2), (-9, 0, -1, 0), (6, 1, 0, 0), (9, 0, 1, 1), (2, 0, 0, 2),
     (-7, 1, -1, 1), (6, 0, 0, 0), (7, 0, 1, 1), (2, 1, 0, 2), (-9, 1, -1, 1), (3, 0, 0, 2), (5, 0, 0, 0),
     (-2, 1, -1, 1), (-6, 0, -1, 1), (-4, 0, 0, 4), (3, 1, 0, 2), (-2, 0, 0, 0), (-5, 0, -1, 1), (-6, 1, 0, 2),
     (4, 1, 0, 0), (-3, 0, 0, 0), (4, 0, 0, 2), (5, 1, 0, 2), (-5, 1, -1, 1), (-3, 1, 0, 0), (-4, 1, -1, 1)),
    ((-8, 0, -1, 2), (-1, 1, 0, 1), (1, 0, 0, 3), (8, 0, 1, 2), (8, 1, 1, 2), (-8, 1, -1, 2), (-1, 0, 0, 1),
     (1, 1, 0, 3), (-7, 0, -1, 3), (2, 0, 0, 3), (-9, 1, -1, 2), (-2, 0, 0, 1), (9, 0, 1, 2), (-9, 0, -1, 2),
     (2, 1, 0, 3), (-2, 1, 0, 1), (7, 0, 1, 2), (-7, 1, -1, 2), (-6, 0, -1, 2), (5, 1, 0, 1), (3, 0, 0, 3),
     (6, 0, 1, 2), (6, 1, 1, 2), (-6, 1, -1, 2), (4, 1, 0, 0), (3, 1, 0, 3), (7, 1, 0, 3), (5, 0, 0, 1),
     (-3, 1, -1, 2), (-5, 0, -1, 2), (4, 0, 0, 1), (-5, 1, 0, 3), (-3, 0, 0, 1), (-4, 1, -1, 3), (-4, 0, 0, 3)),
    ((8, 1, 1, 3), (-8, 0, -1, 3), (1, 0, 0, 4), (-1, 0, 0, 2), (8, 0, 1, 3), (-8, 1, -1, 3), (1, 1, 0, 4),
     (-1, 1, 0, 2), (-7, 0, 0, 4), (-2, 1, 0, 2), (9, 0, 1, 3), (2, 0, 0, 4), (-2, 0, 0, 2), (-7, 1, -1, 3),
     (7, 0, 1, 3), (2, 1, 0, 4), (-9, 0, 0, 1), (7, 1, 1, 3), (-9, 1, -1, 3), (6, 1, 1, 3), (3, 0, 0, 4),
     (-6, 0, -1, 3), (-3, 0, 0, 2), (6, 0, 1, 3), (-6, 1, -1, 3), (-3, 1, 0, 2), (3, 1, 0, 4), (-5, 0, -1, 3),
     (4, 0, 0, 4), (4, 1, 0, 4), (5, 0, 0, 2), (5, 1, 0, 2), (-5, 1, 0, 4), (-4, 0, -1, 2), (-4, 1, 0, 2)),
    ((-8, 0, -1, 4), (-1, 1, 0, 3), (1, 0, 0, 5), (8, 0, 1, 4), (8, 1, 1, 4), (-8, 1, -1, 4), (-1, 0, 0, 3),
     (1, 1, 0, 5), (7, 1, 0, 3), (2, 0, 0, 5), (-9, 1, -1, 4), (-2, 0, 0, 3), (9, 0, 1, 4), (-7, 0, -1, 4),
     (-9, 0, -1, 4), (2, 1, 0, 5), (-2, 1, 0, 3), (7, 0, 1, 4), (-7, 1, -1, 4), (-6, 0, -1, 4), (-3, 1, 0, 3),
     (3, 0, 0, 5), (6, 0, 1, 4), (6, 1, 1, 4), (3, 1, 0, 5), (-6, 1, -1, 4), (-3, 0, 0, 3), (5, 1, 1, 4),
     (-5, 0, 0, 5), (-4, 0, 0, 3), (-5, 1, 0, 5), (5, 0, 0, 3), (4, 1, 1, 5), (-4, 1, 0, 3), (4, 0, 0, 5)),
    ((-8, 0, -1, 5), (8, 1, 1, 5), (1, 0, 0, 6), (-1, 0, 0, 4), (-8, 1, -1, 5), (1, 1, 0, 6), (-1, 1, 0, 4),
     (7, 1, 1, 4), (8, 0, 1, 5), (-2, 1, 0, 4), (2, 0, 0, 6), (9, 0, 1, 5), (-2, 0, 0, 4), (-7, 1, -1, 5),
     (2, 1, 0, 6), (7, 0, 1, 5), (-9, 1, -1, 5), (-4, 0, 0, 7), (6, 1, 1, 5), (-3, 0, 0, 4), (-6, 0, -1, 5),
     (-5, 0, 0, 6), (6, 0, 1, 5), (-3, 1, 0, 4), (-6, 1, -1, 5), (-5, 1, 0, 6), (-7, 0, 0, 4), (3, 1, 0, 6),
     (3, 0, 1, 5), (5, 0, 0, 4), (-9, 0, -1, 1), (-4, 1, 0, 6), (4, 0, 1, 4), (5, 1, 1, 5), (4, 1, 0, 4)),
    ((-8, 0, -1, 6), (-1, 1, 0, 5), (1, 0, 0, 7), (8, 0, 1, 6), (8, 1, 1, 6), (-8, 1, -1, 6), (-1, 0, 0, 5),
     (1, 1, 0, 7), (-9, 0, 0, 5), (7, 1, 0, 5), (-7, 0, 0, 7), (-2, 0, 0, 5), (-9, 1, -1, 6), (-6, 0, 0, 7),
     (9, 0, 1, 6), (-2, 1, 0, 5), (-6, 1, 0, 7), (-7, 1, -1, 6), (7, 0, 1, 6), (-3, 1, 0, 5), (2, 0, 1, 6),
     (2, 1, 0, 7), (6, 1, 1, 6), (-3, 0, 0, 5), (-5, 1, 0, 7), (5, 1, 1, 6), (4, 1, 0, 3), (-4, 0, 0, 7), (6, 0, 0, 5),
     (3, 1, 0, 7), (-5, 0, 0, 5), (5, 0, 1, 6), (-4, 1, 0, 5), (3, 0, 0, 7), (4, 0, 1, 6)),
    ((-8, 0, -1, 7), (-7, 0, 0, 0), (-1, 0, 0, 6), (8, 0, 1, 7), (8, 1, 1, 7), (-7, 1, 0, 0), (-1, 1, 0, 6),
     (-9, 0, -1, 6), (-6, 0, 0, 0), (-8, 1, -1, 7), (-2, 1, 0, 6), (1, 0, 1, 7), (1, 1, 1, 7), (7, 0, 0, 6),
     (-6, 1, 0, 0), (7, 1, 0, 6), (-9, 1, -1, 7), (6, 1, 1, 7), (-2, 0, 0, 6), (-5, 0, 0, 0), (9, 0, 1, 7),
     (2, 1, 1, 7), (-4, 0, 0, 1), (2, 0, 0, 0), (6, 0, 1, 7), (-4, 1, 0, 6), (5, 1, 0, 6), (-5, 1, 0, 0), (3, 0, 1, 7),
     (4, 1, 0, 6), (-3, 1, 0, 0), (4, 0, 1, 7), (-3, 0, 0, 0), (3, 1, 1, 7), (5, 0, 0, 6)),
)


def offset_of(d):
    return (d + 1) // 2


def line_of(y, d):
    return (y + d) // LINE


def needed_tiles(d, part):
    first, last = (0, (2 * HALF - d) // 2) if d > 0 else ((-d) // 2, TILES - 1)
    return max(first, PARTS[part][0]), min(last, PARTS[part][1])


def source_slot(y, d, line, column):
    return d + y - line * LINE - column


def receivers(column, slot, part):
    found = []
    for y in range(LINE):
        for d, piece, line, relay in ROUTES[y]:
            if relay == column and piece == part and source_slot(y, d, line, relay) == slot:
                found.append((y, d, -line))
    return found


@functools.cache
def sent_tiles(y, d, part):
    first, last = needed_tiles(d, part)
    for y_next, d_next, _ in receivers(y, d, part):
        first_next, last_next = sent_tiles(y_next, d_next, part)
        first, last = min(first, first_next), max(last, last_next)
    return first, last


@functools.cache
def depth_of(y, d, part):
    return 1 + max([depth_of(y_next, d_next, part) for y_next, d_next, _ in receivers(y, d, part)], default=0)


def sends_from(column):
    own = [(0, part, *entry) for part in range(2) for entry in receivers(column, 0, part)]
    own.sort(key=lambda entry: -depth_of(entry[2], entry[3], entry[1]))
    relayed = [
        (d, part, *entry) for d, part, _, _ in ROUTES[column] for entry in receivers(column, d, part)
    ]
    return own + relayed


MOST_SENDS = max(len(sends_from(column)) for column in range(LINE))


def partners_of(column):
    found = {(line, relay) for _, _, line, relay in ROUTES[column]}
    return sorted(found | {(line, y) for _, _, y, _, line in sends_from(column)})


def kernel(lines, columns, dens_ref, pat_ref, out_ref, band, shifted, squares, low, send_sem, recv_sem):
    me = lax.axis_index("row") * columns + lax.axis_index("col")
    my_line = me // LINE
    my_column = lax.rem(me, LINE)

    def place(line, y):
        index = (my_line + line) * LINE + y
        return (index // columns, lax.rem(index, columns))

    there = {line: (my_line + line >= 0) & (my_line + line < lines) for line in range(-2, 3)}

    def rows_of(step, d):
        order = (d + HALF - 1) // 2 if d % 2 == 0 else HALF + (d + HALF) // 2
        return pl.ds(pl.multiple_of(step * FULL + order * BLOCK, BLOCK), BLOCK)

    def lanes_of(d, first, last):
        return pl.ds((MARGIN + offset_of(d) + first) * LANES, (last - first + 1) * LANES)

    def copy(step, number, slot, part, y, d, line):
        first, last = sent_tiles(y, d, part)
        return pltpu.make_async_remote_copy(
            src_ref=band.at[rows_of(step, slot), lanes_of(slot, first, last)],
            dst_ref=band.at[rows_of(step, d), lanes_of(d, first, last)],
            send_sem=send_sem.at[step, number],
            recv_sem=recv_sem.at[step, 2 * (d + HALF) + part],
            device_id=place(line, y),
            device_id_type=MESH,
        )

    def arrival(step, y, d, part):
        first, last = sent_tiles(y, d, part)
        piece = band.at[rows_of(step, d), lanes_of(d, first, last)]
        return pltpu.make_async_remote_copy(
            src_ref=piece,
            dst_ref=piece,
            send_sem=send_sem.at[step, 0],
            recv_sem=recv_sem.at[step, 2 * (d + HALF) + part],
            device_id=place(0, y),
            device_id_type=MESH,
        )

    def each_column(body):
        for column in range(LINE):
            pl.when(my_column == column)(functools.partial(body, column))

    def sent_when(column, slot, line):
        return there[line] & there[line_of(column, slot)]

    for step in range(STEPS):
        for d in range(-HALF, HALF + 1):
            off = offset_of(d)
            if d > 0:
                band[rows_of(step, d), MARGIN * LANES:(MARGIN + off) * LANES] = jnp.zeros(
                    (BLOCK, off * LANES), jnp.bfloat16
                )
            elif off < 0:
                band[rows_of(step, d), (MARGIN + TILES + off) * LANES:(MARGIN + TILES) * LANES] = jnp.zeros(
                    (BLOCK, -off * LANES), jnp.bfloat16
                )
            if d != 0:
                @pl.when((me + d < 0) | (me + d >= lines * LINE))
                def _():
                    band[rows_of(step, d), MARGIN * LANES:(MARGIN + TILES) * LANES] = jnp.zeros(
                        (BLOCK, WIDTH), jnp.bfloat16
                    )

    barrier = pltpu.get_barrier_semaphore()

    def greet(column):
        count = jnp.int32(0)
        for line, y in partners_of(column):
            @pl.when(there[line])
            def _():
                pl.semaphore_signal(barrier, inc=1, device_id=place(line, y), device_id_type=MESH)

            count += there[line].astype(jnp.int32)
        pl.semaphore_wait(barrier, count)

    each_column(greet)

    low[0:BLOCK, :] = jnp.zeros((BLOCK, BLOCK), jnp.bfloat16)
    low[(SLOTS + 1) * BLOCK:(SLOTS + 2) * BLOCK, :] = jnp.zeros((BLOCK, BLOCK), jnp.bfloat16)
    squares[(SLOTS + 1) * BLOCK:(SLOTS + 2) * BLOCK, :] = jnp.zeros((BLOCK, BLOCK), jnp.float32)
    squares[0:BLOCK, :] = jnp.zeros((BLOCK, BLOCK), jnp.float32)

    current = dens_ref[...]
    padded = jnp.concatenate(
        [current, jnp.zeros((BLOCK, WIDTH - FULL), jnp.float32)], axis=1
    )
    band[rows_of(0, 0), MARGIN * LANES:(MARGIN + TILES) * LANES] = padded.astype(jnp.bfloat16)
    padded = jnp.concatenate([jnp.zeros((BLOCK, BLOCK), jnp.float32), current], axis=1)
    shifted[...] = padded.astype(jnp.bfloat16)
    window = pl.ds(MARGIN * LANES, WIDTH)

    def purify(step, _):
        def exchange(column):
            sends = sends_from(column)

            def send(slot, part):
                for number, entry in enumerate(sends):
                    if entry[:2] == (slot, part):
                        @pl.when(sent_when(column, slot, entry[4]))
                        def _():
                            copy(step, number, *entry).start()

            for number, entry in enumerate(sends):
                if entry[0] == 0:
                    @pl.when(sent_when(column, 0, entry[4]))
                    def _():
                        copy(step, number, *entry).start()
            for d, part, _, _ in ROUTES[column]:
                @pl.when(there[line_of(column, d)])
                def _():
                    arrival(step, column, d, part).wait_recv()

                send(d, part)

        each_column(exchange)
        own = band[rows_of(step, 0), window]
        even_rows = band[pl.ds(pl.multiple_of(step * FULL, BLOCK), EVENS), window]
        odd_rows = band[pl.ds(pl.multiple_of(step * FULL + EVENS, BLOCK), ODDS), window]
        across = (((1,), (1,)), ((), ()))
        even_square = lax.dot_general(even_rows, own, across, preferred_element_type=jnp.float32)
        odd_square = lax.dot_general(odd_rows, shifted[...], across, preferred_element_type=jnp.float32)
        for slot in range(SLOTS):
            order = (slot - 1) // 2 if slot % 2 else slot // 2
            source = even_square if slot % 2 else odd_square
            kept = pat_ref[0, slot].astype(jnp.float32)
            part = source[order * BLOCK:(order + 1) * BLOCK, :] * kept
            squares[(1 + slot) * BLOCK:(2 + slot) * BLOCK, :] = part
            low[(1 + slot) * BLOCK:(2 + slot) * BLOCK, :] = part.astype(jnp.bfloat16)
        even_cube = jnp.dot(even_rows, low[BLOCK:BLOCK + WIDTH, :], preferred_element_type=jnp.float32)
        odd_cube = jnp.dot(odd_rows, low[0:WIDTH, :], preferred_element_type=jnp.float32)
        for slot in range(SLOTS):
            order = (slot - 1) // 2 if slot % 2 else slot // 2
            source = even_cube if slot % 2 else odd_cube
            kept = pat_ref[0, slot].astype(jnp.float32)
            part = squares[(1 + slot) * BLOCK:(2 + slot) * BLOCK, :]
            cube = source[order * BLOCK:(order + 1) * BLOCK, :]
            squares[(1 + slot) * BLOCK:(2 + slot) * BLOCK, :] = (3.0 * part - 2.0 * cube) * kept

        @pl.when(step < STEPS - 1)
        def _():
            for tile in range(TILES):
                part = squares[(1 + 2 * tile) * BLOCK:(3 + 2 * tile) * BLOCK, :]
                band[rows_of(step + 1, 0), (MARGIN + tile) * LANES:(MARGIN + 1 + tile) * LANES] = part.T.astype(
                    jnp.bfloat16
                )
            for tile in range(TILES):
                part = squares[2 * tile * BLOCK:(2 + 2 * tile) * BLOCK, :]
                shifted[:, tile * LANES:(1 + tile) * LANES] = part.T.astype(jnp.bfloat16)

        return 0

    lax.fori_loop(0, STEPS, purify, 0)

    for tile in range(TILES):
        part = squares[(1 + 2 * tile) * BLOCK:(3 + 2 * tile) * BLOCK, :].T
        wide = min(LANES, FULL - tile * LANES)
        out_ref[:, tile * LANES:tile * LANES + wide] = part[:, :wide]

    def finish(step, _):
        def drain(column):
            for number, entry in enumerate(sends_from(column)):
                @pl.when(sent_when(column, entry[0], entry[4]))
                def _():
                    copy(step, number, *entry).wait_send()

        each_column(drain)
        return 0

    lax.fori_loop(0, STEPS, finish, 0)


def solution(mesh):
    columns = mesh.shape["col"]
    lines = mesh.shape["row"] * columns // LINE

    def local(density, pattern):
        return pl.pallas_call(
            functools.partial(kernel, lines, columns),
            out_shape=jax.ShapeDtypeStruct((BLOCK, FULL), jnp.float32),
            in_specs=[
                pl.BlockSpec(memory_space=pltpu.VMEM),
                pl.BlockSpec(memory_space=pltpu.SMEM),
            ],
            out_specs=pl.BlockSpec(memory_space=pltpu.VMEM),
            scratch_shapes=[
                pltpu.VMEM((STEPS * FULL, STORED * LANES), jnp.bfloat16),
                pltpu.VMEM((BLOCK, WIDTH), jnp.bfloat16),
                pltpu.VMEM(((SLOTS + 2) * BLOCK, BLOCK), jnp.float32),
                pltpu.VMEM(((SLOTS + 2) * BLOCK, BLOCK), jnp.bfloat16),
                pltpu.SemaphoreType.DMA((STEPS, MOST_SENDS)),
                pltpu.SemaphoreType.DMA((STEPS, 2 * SLOTS)),
            ],
            compiler_params=pltpu.CompilerParams(
                collective_id=0, has_side_effects=True, vmem_limit_bytes=40 << 20
            ),
        )(density, pattern)

    placed = (P(("row", "col"), None), P(("row", "col"), None))
    return jax.shard_map(
        local, mesh=mesh, in_specs=placed, out_specs=P(("row", "col"), None), check_vma=False
    )
```

```python
import functools

import jax
import jax.numpy as jnp
from jax import lax
from jax.experimental import pallas as pl
from jax.experimental.pallas import tpu as pltpu
from jax.sharding import PartitionSpec as P

STEPS = 2
BLOCK = 64
HALF = 9
SLOTS = 2 * HALF + 1
LANES = 128
TILES = 10
WIDTH = TILES * LANES
FULL = SLOTS * BLOCK
LINE = 8
EVENS = 9 * BLOCK
ODDS = 10 * BLOCK
MARGIN = 4
STORED = TILES + 9
PARTS = ((0, 3), (4, 6), (7, 9))
MESH = pl.DeviceIdType.MESH

ROUTES = (
    ((1, 1, 0, 1), (7, 0, 0, 7), (8, 0, 1, 0), (-8, 1, -1, 0), (8, 1, 1, 0), (1, 0, 0, 1), (7, 1, 0, 7),
     (-8, 2, -1, 0), (1, 2, 0, 1), (2, 1, 0, 1), (6, 1, 0, 7), (9, 1, 1, 0), (-7, 1, -1, 0), (-1, 1, 0, 7),
     (2, 2, 0, 1), (-1, 0, -1, 0), (9, 0, 1, 0), (-7, 0, -1, 0), (6, 0, 0, 7), (2, 0, 0, 1), (-7, 2, -1, 0),
     (-1, 2, 0, 7), (3, 2, 0, 1), (-6, 1, -1, 0), (-2, 1, 0, 7), (-6, 2, 0, 1), (-9, 1, -1, 0), (4, 2, 0, 2),
     (5, 0, 0, 7), (-2, 0, -1, 0), (-6, 0, -1, 0), (3, 0, 0, 1), (5, 1, 0, 7), (-9, 2, -1, 0), (3, 1, 0, 1),
     (-2, 2, 0, 7), (-5, 2, -1, 0), (-4, 0, -1, 7), (4, 0, 0, 7), (-3, 0, -1, 0), (-4, 2, 0, 2), (-4, 1, 0, 1),
     (-3, 1, -1, 0), (-3, 2, 0, 6), (-5, 0, 0, 1), (4, 1, 0, 7), (-5, 1, -1, 0)),
    ((1, 1, 0, 2), (-1, 0, 0, 0), (-8, 1, -1, 1), (1, 2, 0, 2), (8, 0, 1, 1), (-1, 2, 0, 0), (-8, 2, -1, 1),
     (8, 1, 1, 1), (-1, 1, 0, 0), (1, 0, 0, 2), (9, 1, 1, 1), (-7, 0, -1, 2), (-7, 1, -1, 1), (2, 2, 0, 2),
     (6, 0, 0, 0), (7, 0, 1, 1), (-7, 2, -1, 1), (6, 1, 0, 0), (3, 1, 0, 3), (-9, 2, -1, 1), (7, 1, 1, 1),
     (2, 0, 0, 2), (-9, 1, -1, 1), (5, 1, 0, 0), (2, 1, 0, 2), (9, 0, 1, 1), (-6, 2, -1, 1), (-2, 1, 0, 0),
     (3, 2, 0, 2), (-5, 1, -1, 1), (-2, 0, 0, 0), (-6, 0, -1, 1), (3, 0, 0, 2), (5, 0, 0, 0), (-3, 1, -1, 1),
     (4, 2, 0, 2), (-5, 0, 0, 3), (-2, 2, 0, 0), (-6, 1, -1, 1), (-5, 2, -1, 1), (4, 0, 0, 0), (-4, 0, -1, 2),
     (-4, 1, 0, 2), (4, 1, 0, 0), (-3, 0, -1, 1), (-3, 2, 0, 0), (-4, 2, 0, 2)),
    ((1, 2, 0, 3), (-1, 0, 0, 1), (-8, 1, -1, 2), (1, 0, 0, 3), (-1, 2, 0, 1), (8, 0, 1, 2), (-8, 2, -1, 2),
     (8, 1, 1, 2), (1, 1, 0, 3), (-1, 1, 0, 1), (-7, 2, -1, 2), (-7, 0, -1, 2), (-2, 0, 0, 1), (7, 0, 1, 2),
     (2, 2, 0, 3), (-9, 2, -1, 2), (-2, 2, 0, 1), (-6, 0, -1, 5), (9, 0, 1, 2), (9, 1, 1, 2), (2, 0, 0, 3),
     (-7, 1, -1, 2), (-2, 1, 0, 1), (7, 1, 1, 2), (3, 1, 0, 3), (-9, 1, -1, 2), (3, 2, 0, 3), (5, 0, 0, 1),
     (6, 0, 1, 2), (-6, 2, -1, 2), (5, 1, 0, 1), (6, 1, 1, 2), (3, 0, 0, 3), (2, 1, 0, 1), (-5, 1, -1, 2),
     (4, 2, 0, 3), (-3, 0, -1, 2), (-5, 2, 0, 3), (4, 1, 0, 1), (-5, 0, 0, 3), (-3, 1, -1, 2), (-6, 1, -1, 2),
     (4, 0, 0, 3), (-3, 2, 0, 1), (-4, 0, -1, 1), (-4, 2, 0, 3), (-4, 1, -1, 2)),
    ((-1, 1, 0, 2), (1, 1, 0, 4), (-8, 1, -1, 3), (1, 2, 0, 4), (-1, 0, 0, 2), (8, 0, 1, 3), (-8, 2, -1, 3),
     (8, 1, 1, 3), (-1, 2, 0, 2), (1, 0, 0, 4), (2, 1, 0, 4), (7, 1, 1, 3), (-9, 1, -1, 3), (9, 1, 1, 3),
     (-2, 0, 0, 2), (4, 2, 0, 7), (2, 2, 0, 4), (-7, 1, -1, 3), (-2, 2, 0, 2), (7, 0, 1, 3), (-7, 2, -1, 3),
     (2, 0, 0, 4), (-2, 1, 0, 2), (-7, 0, -1, 3), (9, 0, 1, 3), (3, 2, 0, 4), (-9, 2, -1, 3), (-3, 0, 0, 2),
     (-6, 2, 0, 4), (6, 0, 1, 3), (-6, 1, -1, 3), (-6, 0, -1, 3), (3, 0, 0, 4), (5, 0, 1, 2), (-3, 2, 0, 2),
     (3, 1, 0, 4), (6, 1, 1, 3), (-5, 2, -1, 3), (5, 1, 0, 1), (4, 0, 0, 4), (-3, 1, 0, 2), (-5, 0, 0, 4),
     (-4, 0, -1, 2), (4, 1, 0, 4), (-5, 1, -1, 3), (-4, 1, 0, 1), (-4, 2, 0, 4)),
    ((1, 1, 0, 5), (-1, 0, 0, 3), (-8, 1, -1, 4), (1, 2, 0, 5), (8, 0, 1, 4), (-1, 1, 0, 3), (-8, 2, -1, 4),
     (8, 1, 1, 4), (1, 0, 0, 5), (-1, 2, 0, 3), (9, 1, 1, 4), (2, 2, 0, 5), (-7, 1, -1, 4), (-2, 1, 0, 3),
     (-7, 2, -1, 4), (7, 0, 1, 4), (2, 0, 0, 5), (-2, 0, 0, 3), (7, 1, 1, 4), (-9, 1, -1, 4), (-7, 0, -1, 4),
     (2, 1, 0, 5), (-2, 2, 0, 3), (9, 0, 1, 4), (-9, 2, -1, 4), (6, 1, 1, 4), (-6, 2, -1, 4), (-3, 0, 0, 3),
     (3, 0, 0, 5), (-6, 0, -1, 4), (-3, 2, 0, 3), (3, 1, 0, 5), (-6, 1, -1, 4), (6, 0, 0, 3), (3, 2, 0, 5),
     (-5, 2, -1, 5), (-3, 1, 0, 3), (-5, 0, -1, 4), (-4, 1, 0, 5), (5, 0, 1, 4), (-4, 0, 0, 3), (-5, 1, -1, 4),
     (4, 1, 0, 6), (4, 2, 1, 5), (4, 0, 0, 3), (-4, 2, 0, 3), (5, 1, 1, 4)),
    ((1, 2, 0, 6), (-1, 0, 0, 4), (-8, 1, -1, 5), (1, 0, 0, 6), (8, 0, 1, 5), (-1, 1, 0, 4), (-8, 2, -1, 5),
     (8, 1, 1, 5), (1, 1, 0, 6), (-1, 2, 0, 4), (-7, 2, -1, 5), (-7, 0, -1, 5), (2, 0, 0, 6), (-2, 0, 0, 4),
     (7, 0, 1, 5), (-9, 1, -1, 5), (2, 1, 0, 6), (9, 0, 1, 5), (-7, 1, -1, 5), (2, 2, 0, 6), (-2, 2, 0, 4),
     (7, 1, 1, 5), (9, 1, 1, 5), (-9, 2, -1, 5), (-5, 1, 0, 6), (-3, 1, 0, 4), (-6, 0, -1, 5), (-5, 2, 0, 6),
     (6, 0, 1, 5), (-6, 1, -1, 5), (-5, 0, 0, 6), (-6, 2, -1, 5), (-3, 0, 0, 4), (-4, 1, 0, 6), (3, 1, 1, 5),
     (-3, 2, 0, 4), (-2, 1, 0, 6), (5, 1, 1, 5), (3, 2, 1, 5), (-4, 2, 0, 4), (3, 0, 0, 6), (5, 0, 0, 4),
     (4, 1, 0, 6), (6, 1, 1, 5), (4, 2, 1, 5), (-4, 0, 0, 6), (4, 0, 0, 4)),
    ((1, 0, 0, 7), (-1, 0, 0, 5), (-8, 1, -1, 6), (8, 0, 1, 6), (1, 1, 0, 7), (-1, 1, 0, 5), (-8, 2, -1, 6),
     (8, 1, 1, 6), (1, 2, 0, 7), (-1, 2, 0, 5), (-6, 1, 0, 7), (-2, 0, 0, 5), (9, 0, 1, 6), (-6, 2, 0, 7),
     (-7, 1, -1, 6), (-2, 1, 0, 5), (-6, 0, 0, 7), (7, 0, 1, 6), (-9, 1, -1, 6), (9, 1, 1, 6), (-5, 1, 0, 7),
     (7, 1, 1, 6), (-3, 1, 0, 4), (-7, 2, -1, 6), (-2, 2, 0, 5), (2, 1, 0, 7), (-9, 2, -1, 6), (6, 0, 1, 6),
     (-3, 0, 0, 5), (2, 0, 0, 7), (6, 1, 1, 6), (2, 2, 0, 7), (3, 1, 1, 6), (-4, 0, 0, 4), (-5, 0, 0, 7),
     (-3, 2, 0, 5), (5, 1, 1, 6), (-5, 2, 0, 7), (-7, 0, -1, 4), (-4, 1, 0, 7), (5, 0, 1, 6), (-4, 2, 0, 7),
     (3, 2, 1, 4), (4, 0, 1, 6), (3, 0, 0, 7), (4, 2, 1, 5), (4, 1, 0, 5)),
    ((-1, 1, 0, 6), (-7, 1, 0, 0), (-8, 1, -1, 7), (-7, 2, 0, 0), (8, 0, 1, 7), (-1, 0, 0, 6), (-8, 2, -1, 7),
     (-7, 0, 0, 0), (8, 1, 1, 7), (-1, 2, 0, 6), (-6, 1, 0, 0), (7, 1, 1, 7), (-9, 1, -1, 7), (1, 1, 1, 7),
     (-2, 0, 0, 6), (1, 0, 0, 0), (1, 2, 1, 7), (-6, 0, 0, 0), (-2, 1, 0, 6), (-9, 2, -1, 7), (-6, 2, 0, 0),
     (7, 0, 1, 7), (-2, 2, 0, 6), (9, 1, 1, 7), (-5, 1, 0, 0), (-3, 0, 0, 6), (2, 1, 0, 0), (9, 0, 1, 7),
     (-3, 1, 0, 6), (-5, 2, 0, 0), (6, 1, 1, 7), (6, 0, 0, 6), (2, 2, 1, 7), (2, 0, 0, 0), (-3, 2, 0, 6),
     (3, 1, 1, 7), (-4, 2, 0, 0), (5, 0, 1, 7), (3, 0, 0, 1), (-4, 0, 0, 0), (5, 1, 1, 7), (3, 2, 1, 7),
     (4, 0, 0, 5), (-5, 0, 0, 6), (4, 2, 1, 7), (-4, 1, 0, 0), (4, 1, 0, 6)),
)


def offset_of(d):
    return (d + 1) // 2


def line_of(y, d):
    return (y + d) // LINE


def needed_tiles(d, part):
    first, last = (0, (2 * HALF - d) // 2) if d > 0 else ((-d) // 2, TILES - 1)
    return max(first, PARTS[part][0]), min(last, PARTS[part][1])


def source_slot(y, d, line, column):
    return d + y - line * LINE - column


def receivers(column, slot, part):
    found = []
    for y in range(LINE):
        for d, piece, line, relay in ROUTES[y]:
            if relay == column and piece == part and source_slot(y, d, line, relay) == slot:
                found.append((y, d, -line))
    return found


@functools.cache
def sent_tiles(y, d, part):
    first, last = needed_tiles(d, part)
    for y_next, d_next, _ in receivers(y, d, part):
        first_next, last_next = sent_tiles(y_next, d_next, part)
        first, last = min(first, first_next), max(last, last_next)
    return first, last


@functools.cache
def depth_of(y, d, part):
    return 1 + max([depth_of(y_next, d_next, part) for y_next, d_next, _ in receivers(y, d, part)], default=0)


def sends_from(column):
    own = [(0, part, *entry) for part in range(len(PARTS)) for entry in receivers(column, 0, part)]
    own.sort(key=lambda entry: -depth_of(entry[2], entry[3], entry[1]))
    relayed = [
        (d, part, *entry) for d, part, _, _ in ROUTES[column] for entry in receivers(column, d, part)
    ]
    return own + relayed


MOST_SENDS = max(len(sends_from(column)) for column in range(LINE))


def partners_of(column):
    found = {(line, relay) for _, _, line, relay in ROUTES[column]}
    return sorted(found | {(line, y) for _, _, y, _, line in sends_from(column)})


def kernel(lines, columns, dens_hbm, pat_hbm, out_ref, dens_ref, pat_ref, band, shifted, squares, low, load_sem, send_sem, recv_sem):
    load = pltpu.make_async_copy(dens_hbm, dens_ref, load_sem.at[0])
    load.start()
    load_pattern = pltpu.make_async_copy(pat_hbm, pat_ref, load_sem.at[1])
    load_pattern.start()
    me = lax.axis_index("row") * columns + lax.axis_index("col")
    my_line = me // LINE
    my_column = lax.rem(me, LINE)

    def place(line, y):
        index = (my_line + line) * LINE + y
        return (index // columns, lax.rem(index, columns))

    there = {line: (my_line + line >= 0) & (my_line + line < lines) for line in range(-2, 3)}

    def rows_of(step, d):
        order = (d + HALF - 1) // 2 if d % 2 == 0 else HALF + (d + HALF) // 2
        return pl.ds(pl.multiple_of(step * FULL + order * BLOCK, BLOCK), BLOCK)

    def lanes_of(d, first, last):
        return pl.ds((MARGIN + offset_of(d) + first) * LANES, (last - first + 1) * LANES)

    def copy(step, number, slot, part, y, d, line):
        first, last = sent_tiles(y, d, part)
        return pltpu.make_async_remote_copy(
            src_ref=band.at[rows_of(step, slot), lanes_of(slot, first, last)],
            dst_ref=band.at[rows_of(step, d), lanes_of(d, first, last)],
            send_sem=send_sem.at[step, number],
            recv_sem=recv_sem.at[step, len(PARTS) * (d + HALF) + part],
            device_id=place(line, y),
            device_id_type=MESH,
        )

    def arrival(step, y, d, part):
        first, last = sent_tiles(y, d, part)
        piece = band.at[rows_of(step, d), lanes_of(d, first, last)]
        return pltpu.make_async_remote_copy(
            src_ref=piece,
            dst_ref=piece,
            send_sem=send_sem.at[step, 0],
            recv_sem=recv_sem.at[step, len(PARTS) * (d + HALF) + part],
            device_id=place(0, y),
            device_id_type=MESH,
        )

    def each_column(body):
        for column in range(LINE):
            pl.when(my_column == column)(functools.partial(body, column))

    def sent_when(column, slot, line):
        return there[line] & there[line_of(column, slot)]

    barrier = pltpu.get_barrier_semaphore()

    def greet(column):
        for line, y in partners_of(column):
            @pl.when(there[line])
            def _():
                pl.semaphore_signal(barrier, inc=1, device_id=place(line, y), device_id_type=MESH)

    def meet(column):
        count = jnp.int32(0)
        for line, _ in partners_of(column):
            count += there[line].astype(jnp.int32)
        pl.semaphore_wait(barrier, count)

    each_column(greet)
    load.wait()
    padded = jnp.concatenate([dens_ref[...], jnp.zeros((BLOCK, WIDTH - FULL), jnp.float32)], axis=1)
    band[rows_of(0, 0), MARGIN * LANES:(MARGIN + TILES) * LANES] = padded.astype(jnp.bfloat16)
    each_column(meet)
    load_pattern.wait()

    def clear():
        for step in range(STEPS):
            for d in range(-HALF, HALF + 1):
                off = offset_of(d)
                if d > 0:
                    band[rows_of(step, d), MARGIN * LANES:(MARGIN + off) * LANES] = jnp.zeros(
                        (BLOCK, off * LANES), jnp.bfloat16
                    )
                elif off < 0:
                    band[rows_of(step, d), (MARGIN + TILES + off) * LANES:(MARGIN + TILES) * LANES] = jnp.zeros(
                        (BLOCK, -off * LANES), jnp.bfloat16
                    )
                if d != 0:
                    @pl.when((me + d < 0) | (me + d >= lines * LINE))
                    def _():
                        band[rows_of(step, d), MARGIN * LANES:(MARGIN + TILES) * LANES] = jnp.zeros(
                            (BLOCK, WIDTH), jnp.bfloat16
                        )
        low[0:BLOCK, :] = jnp.zeros((BLOCK, BLOCK), jnp.bfloat16)
        low[(SLOTS + 1) * BLOCK:(SLOTS + 2) * BLOCK, :] = jnp.zeros((BLOCK, BLOCK), jnp.bfloat16)
        squares[(SLOTS + 1) * BLOCK:(SLOTS + 2) * BLOCK, :] = jnp.zeros((BLOCK, BLOCK), jnp.float32)
        squares[0:BLOCK, :] = jnp.zeros((BLOCK, BLOCK), jnp.float32)

    window = pl.ds(MARGIN * LANES, WIDTH)

    def purify(step, _):
        def offer(column):
            for number, entry in enumerate(sends_from(column)):
                if entry[0] == 0:
                    @pl.when(sent_when(column, 0, entry[4]))
                    def _():
                        copy(step, number, *entry).start()

        def relay(column):
            sends = sends_from(column)
            for d, part, _, _ in ROUTES[column]:
                @pl.when(there[line_of(column, d)])
                def _():
                    arrival(step, column, d, part).wait_recv()

                for number, entry in enumerate(sends):
                    if entry[:2] == (d, part):
                        @pl.when(sent_when(column, d, entry[4]))
                        def _():
                            copy(step, number, *entry).start()

        each_column(offer)

        @pl.when(step == 0)
        def _():
            clear()
            padded = jnp.concatenate([jnp.zeros((BLOCK, BLOCK), jnp.float32), dens_ref[...]], axis=1)
            shifted[...] = padded.astype(jnp.bfloat16)

        @pl.when(step > 0)
        def _():
            for tile in range(TILES):
                part = squares[2 * tile * BLOCK:(2 + 2 * tile) * BLOCK, :]
                shifted[:, tile * LANES:(1 + tile) * LANES] = part.T.astype(jnp.bfloat16)

        each_column(relay)
        own = band[rows_of(step, 0), window]
        even_rows = band[pl.ds(pl.multiple_of(step * FULL, BLOCK), EVENS), window]
        odd_rows = band[pl.ds(pl.multiple_of(step * FULL + EVENS, BLOCK), ODDS), window]
        across = (((1,), (1,)), ((), ()))
        even_square = lax.dot_general(even_rows, own, across, preferred_element_type=jnp.float32)
        odd_square = lax.dot_general(odd_rows, shifted[...], across, preferred_element_type=jnp.float32)
        for slot in range(SLOTS):
            order = (slot - 1) // 2 if slot % 2 else slot // 2
            source = even_square if slot % 2 else odd_square
            kept = pat_ref[0, slot].astype(jnp.float32)
            part = source[order * BLOCK:(order + 1) * BLOCK, :] * kept
            squares[(1 + slot) * BLOCK:(2 + slot) * BLOCK, :] = part
            low[(1 + slot) * BLOCK:(2 + slot) * BLOCK, :] = part.astype(jnp.bfloat16)
        even_cube = jnp.dot(even_rows, low[BLOCK:BLOCK + WIDTH, :], preferred_element_type=jnp.float32)
        odd_cube = jnp.dot(odd_rows, low[0:WIDTH, :], preferred_element_type=jnp.float32)
        for slot in range(SLOTS):
            order = (slot - 1) // 2 if slot % 2 else slot // 2
            source = even_cube if slot % 2 else odd_cube
            kept = pat_ref[0, slot].astype(jnp.float32)
            part = squares[(1 + slot) * BLOCK:(2 + slot) * BLOCK, :]
            cube = source[order * BLOCK:(order + 1) * BLOCK, :]
            squares[(1 + slot) * BLOCK:(2 + slot) * BLOCK, :] = (3.0 * part - 2.0 * cube) * kept

        @pl.when(step < STEPS - 1)
        def _():
            for tile in range(TILES):
                part = squares[(1 + 2 * tile) * BLOCK:(3 + 2 * tile) * BLOCK, :]
                band[rows_of(step + 1, 0), (MARGIN + tile) * LANES:(MARGIN + 1 + tile) * LANES] = part.T.astype(
                    jnp.bfloat16
                )

        return 0

    lax.fori_loop(0, STEPS, purify, 0)

    for tile in range(TILES):
        part = squares[(1 + 2 * tile) * BLOCK:(3 + 2 * tile) * BLOCK, :].T
        wide = min(LANES, FULL - tile * LANES)
        out_ref[:, tile * LANES:tile * LANES + wide] = part[:, :wide]

    def finish(step, _):
        def drain(column):
            for number, entry in enumerate(sends_from(column)):
                @pl.when(sent_when(column, entry[0], entry[4]))
                def _():
                    copy(step, number, *entry).wait_send()

        each_column(drain)
        return 0

    lax.fori_loop(0, STEPS, finish, 0)


def solution(mesh):
    columns = mesh.shape["col"]
    lines = mesh.shape["row"] * columns // LINE

    def local(density, pattern):
        return pl.pallas_call(
            functools.partial(kernel, lines, columns),
            out_shape=jax.ShapeDtypeStruct((BLOCK, FULL), jnp.float32),
            in_specs=[
                pl.BlockSpec(memory_space=pltpu.HBM),
                pl.BlockSpec(memory_space=pltpu.HBM),
            ],
            out_specs=pl.BlockSpec(memory_space=pltpu.VMEM),
            scratch_shapes=[
                pltpu.VMEM((BLOCK, FULL), jnp.float32),
                pltpu.SMEM((1, SLOTS), jnp.int32),
                pltpu.VMEM((STEPS * FULL, STORED * LANES), jnp.bfloat16),
                pltpu.VMEM((BLOCK, WIDTH), jnp.bfloat16),
                pltpu.VMEM(((SLOTS + 2) * BLOCK, BLOCK), jnp.float32),
                pltpu.VMEM(((SLOTS + 2) * BLOCK, BLOCK), jnp.bfloat16),
                pltpu.SemaphoreType.DMA((2,)),
                pltpu.SemaphoreType.DMA((STEPS, MOST_SENDS)),
                pltpu.SemaphoreType.DMA((STEPS, len(PARTS) * SLOTS)),
            ],
            compiler_params=pltpu.CompilerParams(
                collective_id=0, has_side_effects=True, vmem_limit_bytes=40 << 20
            ),
        )(density, pattern)

    placed = (P(("row", "col"), None), P(("row", "col"), None))
    return jax.shard_map(
        local, mesh=mesh, in_specs=placed, out_specs=P(("row", "col"), None), check_vma=False
    )
```

```python
import functools

import jax
import jax.numpy as jnp
from jax import lax
from jax.experimental import pallas as pl
from jax.experimental.pallas import tpu as pltpu
from jax.sharding import PartitionSpec as P

STEPS = 2
BLOCK = 64
HALF = 9
SLOTS = 2 * HALF + 1
LANES = 128
TILES = 10
WIDTH = TILES * LANES
FULL = SLOTS * BLOCK
LINE = 8
EVENS = 9 * BLOCK
ODDS = 10 * BLOCK
MARGIN = 4
STORED = TILES + 9
PARTS = ((0, 1), (2, 3), (4, 5), (6, 7), (8, 9))
DELAY = 20
MESH = pl.DeviceIdType.MESH

ROUTES = (
    ((1, 3, 0, 1), (7, 0, 0, 7), (8, 0, 1, 0), (1, 0, 0, 1), (7, 1, 0, 7), (8, 1, 1, 0), (1, 1, 0, 1),
     (7, 2, 0, 7), (-8, 3, -1, 0), (8, 2, 1, 0), (1, 2, 0, 1), (-8, 2, -1, 0), (1, 4, 0, 1), (-8, 4, -1, 0),
     (-1, 4, 0, 7), (2, 1, 0, 1), (-7, 3, -1, 0), (6, 1, 0, 7), (9, 0, 1, 0), (2, 2, 0, 1), (-1, 0, -1, 0),
     (6, 0, 0, 7), (9, 1, 1, 0), (2, 3, 0, 1), (-1, 1, -1, 0), (-1, 3, 0, 7), (-7, 1, -1, 0), (9, 2, 1, 0),
     (2, 4, 0, 1), (6, 2, 0, 7), (-7, 2, -1, 0), (2, 0, 0, 1), (-1, 2, 0, 7), (-7, 4, -1, 0), (3, 1, 0, 1),
     (6, 3, 0, 7), (-9, 4, -1, 0), (5, 2, 0, 7), (-6, 1, -1, 0), (-6, 2, 0, 1), (5, 3, 0, 7), (-2, 1, -1, 0),
     (-2, 0, -1, 0), (-2, 2, 0, 7), (3, 0, 0, 1), (-6, 3, -1, 0), (5, 0, 0, 7), (4, 1, 0, 1), (-9, 3, -1, 0),
     (5, 1, 0, 7), (-5, 1, 0, 1), (-6, 4, -1, 0), (-2, 3, 0, 7), (4, 2, 0, 1), (-9, 2, -1, 0), (-2, 4, 0, 7),
     (-5, 3, 0, 1), (-3, 2, -1, 0), (4, 3, 0, 7), (-5, 2, 0, 1), (-3, 3, -1, 0), (4, 0, 0, 7), (-3, 0, -1, 0),
     (3, 2, 0, 7), (-4, 1, -1, 0), (-4, 4, 0, 2), (-5, 4, 0, 1), (3, 3, 0, 7), (-3, 1, -1, 0), (-3, 4, 0, 2),
     (-4, 2, 0, 1), (-4, 3, -1, 0)),
    ((-1, 2, 0, 0), (1, 1, 0, 2), (-1, 0, 0, 0), (1, 2, 0, 2), (-1, 1, 0, 0), (1, 3, 0, 2), (-8, 2, -1, 1),
     (8, 0, 1, 1), (-1, 3, 0, 0), (1, 4, 0, 2), (-8, 3, -1, 1), (8, 1, 1, 1), (-1, 4, 0, 0), (1, 0, 0, 2),
     (-8, 4, -1, 1), (8, 2, 1, 1), (2, 1, 0, 2), (-9, 2, -1, 1), (6, 3, 0, 7), (6, 0, 0, 0), (-7, 1, -1, 1),
     (7, 2, 1, 1), (2, 2, 0, 2), (6, 1, 0, 0), (-7, 2, -1, 1), (9, 1, 1, 1), (2, 3, 0, 2), (6, 2, 0, 0),
     (-7, 3, -1, 1), (7, 0, 1, 1), (2, 4, 0, 2), (9, 2, 1, 1), (-9, 3, 0, 0), (-7, 4, -1, 1), (2, 0, 0, 2),
     (7, 1, 1, 1), (-2, 4, 0, 0), (-9, 4, -1, 1), (3, 1, 0, 2), (9, 0, 1, 1), (5, 1, 0, 0), (-6, 1, -1, 1),
     (3, 2, 0, 2), (-2, 0, -1, 1), (5, 0, 0, 0), (-6, 3, 0, 2), (-6, 2, -1, 1), (-2, 3, 0, 0), (3, 3, 0, 2),
     (-2, 1, -1, 1), (5, 2, 0, 0), (3, 0, 0, 2), (-2, 2, -1, 1), (-6, 4, -1, 1), (4, 1, 0, 2), (4, 2, 0, 0),
     (-5, 1, -1, 1), (4, 3, 0, 0), (-5, 2, 0, 2), (-3, 1, -1, 1), (-3, 0, 0, 0), (-5, 3, -1, 1), (-3, 2, 0, 0),
     (4, 0, 0, 0), (-5, 4, 0, 2), (5, 3, 0, 2), (-4, 1, -1, 0), (-4, 2, -1, 1), (-3, 3, 0, 0), (-4, 3, -1, 1),
     (-3, 4, 0, 0), (-4, 4, 0, 2)),
    ((1, 1, 0, 3), (-1, 0, 0, 1), (1, 2, 0, 3), (-1, 1, 0, 1), (1, 3, 0, 3), (-8, 2, -1, 2), (-1, 2, 0, 1),
     (8, 0, 1, 2), (1, 4, 0, 3), (-8, 3, -1, 2), (-1, 3, 0, 1), (8, 1, 1, 2), (1, 0, 0, 3), (-8, 4, -1, 2),
     (-1, 4, 0, 1), (-7, 1, -1, 2), (8, 2, 1, 2), (2, 1, 0, 3), (-2, 2, 0, 1), (9, 1, 1, 2), (-7, 2, -1, 2),
     (2, 2, 0, 3), (-2, 0, 0, 1), (7, 0, 1, 2), (-7, 3, -1, 2), (2, 3, 0, 3), (9, 2, 1, 2), (-2, 1, 0, 1),
     (-9, 2, -1, 2), (2, 4, 0, 3), (7, 1, 1, 2), (-2, 3, 0, 1), (-7, 4, -1, 2), (2, 0, 0, 3), (7, 2, 1, 2),
     (-2, 4, 0, 1), (5, 3, 0, 1), (-9, 3, -1, 2), (9, 0, 1, 2), (3, 1, 0, 3), (5, 0, 0, 1), (-9, 4, -1, 2),
     (6, 2, 1, 2), (-6, 1, -1, 2), (3, 2, 0, 3), (5, 1, 0, 1), (6, 0, 1, 2), (-6, 2, -1, 2), (3, 3, 0, 3),
     (5, 2, 0, 1), (6, 1, 1, 2), (-6, 3, -1, 2), (3, 0, 0, 3), (6, 3, 1, 2), (-3, 4, 0, 1), (-6, 4, -1, 2),
     (4, 2, 0, 3), (4, 1, 0, 1), (-5, 1, -1, 2), (-3, 0, 0, 1), (4, 3, 0, 3), (-5, 2, -1, 2), (-5, 4, 0, 3),
     (4, 0, 0, 1), (-3, 1, -1, 2), (-3, 3, 0, 1), (-5, 3, -1, 2), (-3, 2, -1, 2), (-4, 4, 0, 3), (-4, 2, -1, 2),
     (-4, 1, -1, 2), (-4, 3, -1, 2)),
    ((1, 1, 0, 4), (-1, 0, 0, 2), (1, 2, 0, 4), (-1, 1, 0, 2), (1, 3, 0, 4), (-8, 2, -1, 3), (-1, 2, 0, 2),
     (8, 0, 1, 3), (1, 4, 0, 4), (-8, 3, -1, 3), (-1, 3, 0, 2), (8, 1, 1, 3), (1, 0, 0, 4), (-8, 4, -1, 3),
     (-1, 4, 0, 2), (-7, 1, -1, 3), (8, 2, 1, 3), (2, 4, 0, 4), (-2, 0, 0, 2), (9, 1, 1, 3), (-7, 2, -1, 3),
     (2, 1, 0, 4), (-2, 1, 0, 2), (7, 0, 1, 3), (-7, 3, -1, 3), (2, 2, 0, 4), (9, 2, 1, 3), (-2, 2, 0, 2),
     (-9, 2, -1, 3), (2, 3, 0, 4), (7, 1, 1, 3), (-2, 3, 0, 2), (-7, 4, -1, 3), (2, 0, 0, 4), (7, 2, 1, 3),
     (-2, 4, 0, 2), (-9, 3, -1, 3), (3, 2, 0, 4), (9, 0, 1, 3), (-3, 2, 0, 2), (-9, 4, -1, 3), (3, 3, 0, 4),
     (6, 0, 1, 3), (-3, 0, 0, 2), (-6, 4, -1, 3), (3, 1, 0, 4), (6, 1, 1, 3), (-6, 1, -1, 3), (-3, 1, 0, 2),
     (6, 2, 1, 3), (-6, 2, -1, 3), (-3, 3, 0, 2), (6, 3, 1, 3), (3, 0, 0, 4), (-5, 4, -1, 4), (5, 2, 1, 3),
     (-6, 3, -1, 3), (4, 0, 0, 2), (4, 1, 0, 4), (-5, 2, -1, 3), (5, 0, 0, 2), (5, 1, 1, 3), (5, 3, 1, 3),
     (4, 2, 0, 2), (-4, 1, -1, 4), (-5, 3, -1, 3), (-4, 4, 0, 2), (4, 3, 0, 4), (-3, 4, 0, 4), (-4, 2, -1, 4),
     (-5, 1, -1, 3), (-4, 3, -1, 4)),
    ((1, 4, 0, 5), (-1, 2, 0, 3), (1, 1, 0, 5), (-1, 3, 0, 3), (1, 2, 0, 5), (-8, 2, -1, 4), (-1, 0, 0, 3),
     (8, 0, 1, 4), (1, 3, 0, 5), (-8, 3, -1, 4), (-1, 1, 0, 3), (8, 1, 1, 4), (1, 0, 0, 5), (-8, 4, -1, 4),
     (-1, 4, 0, 3), (8, 2, 1, 4), (2, 2, 0, 5), (-7, 4, -1, 4), (-2, 0, 0, 3), (7, 2, 1, 4), (2, 3, 0, 5),
     (-9, 2, -1, 4), (-2, 1, 0, 3), (-7, 1, -1, 4), (9, 1, 1, 4), (2, 1, 0, 5), (9, 2, 1, 4), (-2, 2, 0, 3),
     (-9, 3, -1, 4), (2, 4, 0, 5), (7, 0, 1, 4), (-2, 3, 0, 3), (-7, 2, -1, 4), (2, 0, 0, 5), (7, 1, 1, 4),
     (-2, 4, 0, 3), (-7, 3, -1, 4), (9, 0, 1, 4), (-3, 0, 0, 3), (3, 1, 0, 5), (-9, 4, -1, 4), (6, 0, 1, 4),
     (-3, 1, 0, 3), (3, 2, 0, 5), (-6, 2, -1, 4), (6, 1, 1, 4), (-3, 2, 0, 3), (3, 3, 0, 5), (-6, 3, -1, 4),
     (-6, 1, -1, 4), (6, 2, 1, 4), (-3, 3, 0, 3), (3, 0, 0, 5), (6, 3, 1, 4), (-6, 4, -1, 4), (-3, 4, 0, 3),
     (5, 0, 1, 4), (-4, 4, 0, 5), (-5, 4, -1, 5), (-5, 1, -1, 4), (-4, 2, 0, 5), (4, 2, 1, 3), (5, 1, 1, 4),
     (-5, 2, -1, 4), (-4, 1, 0, 3), (-5, 3, -1, 4), (4, 0, 1, 3), (5, 2, 1, 4), (-4, 3, 0, 3), (5, 3, 1, 4),
     (4, 1, 1, 3), (4, 3, 1, 3)),
    ((1, 2, 0, 6), (-1, 3, 0, 4), (1, 3, 0, 6), (-1, 0, 0, 4), (1, 1, 0, 6), (-8, 2, -1, 5), (-1, 1, 0, 4),
     (8, 0, 1, 5), (1, 4, 0, 6), (-8, 3, -1, 5), (-1, 2, 0, 4), (8, 1, 1, 5), (1, 0, 0, 6), (-8, 4, -1, 5),
     (-1, 4, 0, 4), (8, 2, 1, 5), (-7, 2, -1, 5), (9, 2, 1, 5), (-2, 2, 0, 4), (2, 1, 0, 6), (-9, 3, -1, 5),
     (7, 0, 1, 5), (-2, 3, 0, 4), (2, 2, 0, 6), (-7, 3, -1, 5), (9, 1, 1, 5), (-2, 0, 0, 4), (2, 3, 0, 6),
     (-7, 1, -1, 5), (7, 1, 1, 5), (-2, 1, 0, 4), (2, 0, 0, 6), (-7, 4, -1, 5), (7, 2, 1, 5), (-2, 4, 0, 4),
     (2, 4, 0, 6), (-9, 2, -1, 5), (9, 0, 1, 5), (-3, 0, 0, 4), (-5, 4, 0, 6), (-9, 4, -1, 5), (-6, 1, -1, 5),
     (6, 2, 1, 5), (-3, 1, 0, 4), (-5, 2, 0, 6), (6, 3, 1, 5), (-6, 2, -1, 5), (-3, 2, 0, 4), (-5, 3, 0, 6),
     (6, 0, 1, 5), (-6, 3, -1, 5), (-3, 3, 0, 4), (6, 1, 1, 5), (-3, 4, 0, 4), (-6, 4, -1, 5), (-5, 1, 0, 6),
     (5, 0, 1, 5), (-4, 3, 0, 6), (-4, 1, 0, 4), (5, 1, 1, 5), (3, 0, 0, 6), (-4, 2, 0, 4), (5, 2, 1, 5),
     (3, 1, 0, 6), (3, 3, 1, 5), (5, 3, 1, 5), (-4, 4, 0, 6), (4, 0, 0, 4), (4, 3, 1, 5), (4, 1, 1, 5),
     (3, 2, 0, 4), (4, 2, 1, 5)),
    ((-1, 2, 0, 5), (1, 1, 0, 7), (-1, 3, 0, 5), (1, 2, 0, 7), (-8, 2, -1, 6), (-1, 0, 0, 5), (8, 0, 1, 6),
     (1, 3, 0, 7), (-8, 3, -1, 6), (-1, 1, 0, 5), (8, 1, 1, 6), (1, 0, 0, 7), (-8, 4, -1, 6), (-1, 4, 0, 5),
     (8, 2, 1, 6), (1, 4, 0, 7), (-9, 2, -1, 6), (-2, 3, 0, 5), (-7, 1, -1, 6), (7, 2, 1, 6), (-6, 4, 0, 7),
     (-2, 0, 0, 5), (9, 2, 1, 6), (-9, 3, -1, 6), (-6, 2, 0, 7), (7, 0, 1, 6), (-2, 1, 0, 5), (-7, 2, -1, 6),
     (-6, 3, 0, 7), (7, 1, 1, 6), (-2, 2, 0, 5), (-7, 3, -1, 6), (9, 1, 0, 7), (9, 0, 1, 6), (-2, 4, 0, 5),
     (-9, 4, -1, 6), (-6, 1, 0, 7), (6, 3, 1, 6), (2, 4, 1, 6), (-3, 2, 0, 5), (-7, 4, -1, 6), (-5, 3, 0, 7),
     (6, 0, 1, 6), (-3, 3, 0, 5), (2, 0, 0, 7), (2, 2, 1, 6), (-3, 0, 0, 5), (2, 1, 0, 7), (2, 3, 1, 6),
     (6, 1, 0, 5), (-5, 2, 0, 7), (6, 2, 1, 6), (-3, 1, 0, 5), (-5, 4, 0, 7), (-3, 4, 0, 5), (3, 3, 1, 6),
     (-4, 1, 0, 7), (5, 3, 1, 6), (5, 2, 0, 5), (3, 0, 0, 7), (5, 0, 1, 6), (-4, 2, 0, 7), (-4, 3, 0, 5),
     (3, 1, 0, 7), (5, 1, 1, 6), (4, 0, 0, 5), (3, 2, 0, 7), (4, 3, 1, 7), (4, 1, 1, 6), (-5, 1, 0, 5),
     (-4, 4, 0, 7), (4, 2, 1, 6)),
    ((-8, 4, -1, 7), (-7, 4, 0, 0), (-1, 1, 0, 6), (-1, 0, 0, 6), (-8, 3, -1, 7), (-7, 2, 0, 0), (-1, 2, 0, 6),
     (-8, 2, -1, 7), (-7, 3, 0, 0), (8, 1, 1, 7), (-1, 3, 0, 6), (-7, 1, 0, 0), (8, 0, 1, 7), (-1, 4, 0, 6),
     (8, 2, 1, 7), (-6, 3, 0, 0), (1, 4, 1, 7), (-2, 2, 0, 6), (1, 0, 0, 0), (7, 1, 1, 7), (-2, 3, 0, 6),
     (1, 1, 0, 0), (7, 0, 1, 7), (-9, 2, -1, 7), (-6, 1, 0, 0), (-2, 0, 0, 6), (7, 2, 1, 7), (1, 2, 0, 0),
     (-2, 1, 0, 6), (-9, 3, -1, 7), (1, 3, 1, 7), (-6, 2, 0, 0), (-2, 4, 0, 6), (-9, 4, -1, 7), (2, 3, 1, 7),
     (-6, 4, 0, 0), (-3, 3, 0, 6), (6, 2, 1, 7), (-5, 1, 0, 0), (-3, 0, 0, 6), (9, 0, 1, 7), (2, 0, 0, 0),
     (6, 3, 1, 7), (-5, 2, 0, 0), (9, 1, 1, 7), (-3, 4, 0, 6), (2, 1, 0, 0), (6, 0, 1, 7), (5, 3, 0, 6),
     (9, 2, 1, 7), (-5, 3, 0, 0), (-4, 2, 0, 6), (6, 1, 1, 7), (2, 2, 0, 0), (2, 4, 1, 7), (-4, 3, 0, 6),
     (-5, 4, 0, 0), (3, 1, 1, 7), (-4, 1, 0, 0), (4, 0, 0, 5), (5, 0, 1, 7), (5, 1, 0, 6), (-3, 1, 0, 0),
     (3, 2, 1, 7), (5, 2, 0, 6), (3, 3, 1, 7), (-3, 2, 0, 0), (3, 0, 0, 5), (4, 3, 1, 7), (-4, 4, 0, 6),
     (4, 2, 0, 6), (4, 1, 1, 7)),
)


def offset_of(d):
    return (d + 1) // 2


def line_of(y, d):
    return (y + d) // LINE


def needed_tiles(d, part):
    first, last = (0, (2 * HALF - d) // 2) if d > 0 else ((-d) // 2, TILES - 1)
    return max(first, PARTS[part][0]), min(last, PARTS[part][1])


def source_slot(y, d, line, column):
    return d + y - line * LINE - column


def receivers(column, slot, part):
    found = []
    for y in range(LINE):
        for d, piece, line, relay in ROUTES[y]:
            if relay == column and piece == part and source_slot(y, d, line, relay) == slot:
                found.append((y, d, -line))
    return found


@functools.cache
def sent_tiles(y, d, part):
    first, last = needed_tiles(d, part)
    for y_next, d_next, _ in receivers(y, d, part):
        first_next, last_next = sent_tiles(y_next, d_next, part)
        first, last = min(first, first_next), max(last, last_next)
    return first, last


@functools.cache
def depth_of(y, d, part):
    return 1 + max([depth_of(y_next, d_next, part) for y_next, d_next, _ in receivers(y, d, part)], default=0)


@functools.cache
def sends_from(column):
    own = [(0, part, *entry) for part in range(len(PARTS)) for entry in receivers(column, 0, part)]
    own.sort(key=lambda entry: -depth_of(entry[2], entry[3], entry[1]))
    relayed = [
        (d, part, *entry) for d, part, _, _ in ROUTES[column] for entry in receivers(column, d, part)
    ]
    return own + relayed


def turn_of(column, slot, part):
    return max([0] + [turn for turn, entry in enumerate(ROUTES[column]) if entry[:2] == (slot, part)])


def sent_before(column, first, last):
    return [
        number
        for number, entry in enumerate(sends_from(column))
        if first <= turn_of(column, entry[0], entry[1]) < last
    ]


def even_turns(column):
    return 1 + max(turn for turn, entry in enumerate(ROUTES[column]) if entry[0] % 2 == 0)


MOST_SENDS = max(len(sends_from(column)) for column in range(LINE))


def partners_of(column):
    found = {(line, relay) for _, _, line, relay in ROUTES[column]}
    return sorted(found | {(line, y) for _, _, y, _, line in sends_from(column)})


def kernel(lines, columns, dens_hbm, pat_hbm, out_ref, dens_ref, pat_ref, band, shifted, squares, low, load_sem, send_sem, recv_sem):
    load = pltpu.make_async_copy(dens_hbm, dens_ref, load_sem.at[0])
    load.start()
    load_pattern = pltpu.make_async_copy(pat_hbm, pat_ref, load_sem.at[1])
    load_pattern.start()
    me = lax.axis_index("row") * columns + lax.axis_index("col")
    my_line = me // LINE
    my_column = lax.rem(me, LINE)

    def place(line, y):
        index = (my_line + line) * LINE + y
        return (index // columns, lax.rem(index, columns))

    there = {line: (my_line + line >= 0) & (my_line + line < lines) for line in range(-2, 3)}

    def rows_of(step, d):
        order = (d + HALF - 1) // 2 if d % 2 == 0 else HALF + (d + HALF) // 2
        return pl.ds(pl.multiple_of(step * FULL + order * BLOCK, BLOCK), BLOCK)

    def lanes_of(d, first, last):
        return pl.ds((MARGIN + offset_of(d) + first) * LANES, (last - first + 1) * LANES)

    def copy(step, number, slot, part, y, d, line):
        first, last = sent_tiles(y, d, part)
        return pltpu.make_async_remote_copy(
            src_ref=band.at[rows_of(step, slot), lanes_of(slot, first, last)],
            dst_ref=band.at[rows_of(step, d), lanes_of(d, first, last)],
            send_sem=send_sem.at[step, number],
            recv_sem=recv_sem.at[step, len(PARTS) * (d + HALF) + part],
            device_id=place(line, y),
            device_id_type=MESH,
        )

    def arrival(step, y, d, part):
        first, last = sent_tiles(y, d, part)
        piece = band.at[rows_of(step, d), lanes_of(d, first, last)]
        return pltpu.make_async_remote_copy(
            src_ref=piece,
            dst_ref=piece,
            send_sem=send_sem.at[step, 0],
            recv_sem=recv_sem.at[step, len(PARTS) * (d + HALF) + part],
            device_id=place(0, y),
            device_id_type=MESH,
        )

    def each_column(body):
        for column in range(LINE):
            pl.when(my_column == column)(functools.partial(body, column))

    def sent_when(column, slot, line):
        return there[line] & there[line_of(column, slot)]

    barrier = pltpu.get_barrier_semaphore()

    def greet(column):
        for line, y in partners_of(column):
            @pl.when(there[line])
            def _():
                pl.semaphore_signal(barrier, inc=1, device_id=place(line, y), device_id_type=MESH)

    def meet(column):
        count = jnp.int32(0)
        for line, _ in partners_of(column):
            count += there[line].astype(jnp.int32)
        pl.semaphore_wait(barrier, count)

    each_column(greet)
    load.wait()
    padded = jnp.concatenate([dens_ref[...], jnp.zeros((BLOCK, WIDTH - FULL), jnp.float32)], axis=1)
    band[rows_of(0, 0), MARGIN * LANES:(MARGIN + TILES) * LANES] = padded.astype(jnp.bfloat16)
    each_column(meet)
    load_pattern.wait()

    def clear():
        for step in range(STEPS):
            for d in range(-HALF, HALF + 1):
                off = offset_of(d)
                if d > 0:
                    band[rows_of(step, d), MARGIN * LANES:(MARGIN + off) * LANES] = jnp.zeros(
                        (BLOCK, off * LANES), jnp.bfloat16
                    )
                elif off < 0:
                    band[rows_of(step, d), (MARGIN + TILES + off) * LANES:(MARGIN + TILES) * LANES] = jnp.zeros(
                        (BLOCK, -off * LANES), jnp.bfloat16
                    )
                if d != 0:
                    @pl.when((me + d < 0) | (me + d >= lines * LINE))
                    def _():
                        band[rows_of(step, d), MARGIN * LANES:(MARGIN + TILES) * LANES] = jnp.zeros(
                            (BLOCK, WIDTH), jnp.bfloat16
                        )
        low[0:BLOCK, :] = jnp.zeros((BLOCK, BLOCK), jnp.bfloat16)
        low[(SLOTS + 1) * BLOCK:(SLOTS + 2) * BLOCK, :] = jnp.zeros((BLOCK, BLOCK), jnp.bfloat16)
        squares[(SLOTS + 1) * BLOCK:(SLOTS + 2) * BLOCK, :] = jnp.zeros((BLOCK, BLOCK), jnp.float32)
        squares[0:BLOCK, :] = jnp.zeros((BLOCK, BLOCK), jnp.float32)

    window = pl.ds(MARGIN * LANES, WIDTH)

    def keep_squares(product, odd):
        for order, slot in enumerate(range(odd, SLOTS, 2)):
            kept = pat_ref[0, slot].astype(jnp.float32)
            part = product[order * BLOCK:(order + 1) * BLOCK, :] * kept
            squares[(1 + slot) * BLOCK:(2 + slot) * BLOCK, :] = part
            low[(1 + slot) * BLOCK:(2 + slot) * BLOCK, :] = part.astype(jnp.bfloat16)

    def drain(step, column, number):
        entry = sends_from(column)[number]

        @pl.when(sent_when(column, entry[0], entry[4]))
        def _():
            copy(step, number, *entry).wait_send()

    def purify(step, _):
        def offer(column):
            for number, entry in enumerate(sends_from(column)):
                if entry[0] == 0:
                    @pl.when(sent_when(column, entry[0], entry[4]))
                    def _():
                        copy(step, number, *entry).start()

        def relay(column, first, last):
            sends = sends_from(column)
            for turn, (d, part, _, _) in enumerate(ROUTES[column]):
                if not first <= turn < last:
                    continue

                @pl.when(there[line_of(column, d)])
                def _():
                    arrival(step, column, d, part).wait_recv()

                for number, entry in enumerate(sends):
                    if entry[:2] == (d, part):
                        @pl.when(sent_when(column, d, entry[4]))
                        def _():
                            copy(step, number, *entry).start()

                for number in sent_before(column, turn - DELAY, turn - DELAY + 1):
                    drain(step, column, number)

        def relay_even(column):
            relay(column, 0, even_turns(column))

        def relay_odd(column):
            relay(column, even_turns(column), len(ROUTES[column]))

        each_column(offer)

        @pl.when(step == 0)
        def _():
            clear()
            padded = jnp.concatenate([jnp.zeros((BLOCK, BLOCK), jnp.float32), dens_ref[...]], axis=1)
            shifted[...] = padded.astype(jnp.bfloat16)

        @pl.when(step > 0)
        def _():
            for tile in range(TILES):
                part = squares[2 * tile * BLOCK:(2 + 2 * tile) * BLOCK, :]
                shifted[:, tile * LANES:(1 + tile) * LANES] = part.T.astype(jnp.bfloat16)

        each_column(relay_even)
        own = band[rows_of(step, 0), window]
        even_rows = band[pl.ds(pl.multiple_of(step * FULL, BLOCK), EVENS), window]
        across = (((1,), (1,)), ((), ()))
        even_square = lax.dot_general(even_rows, own, across, preferred_element_type=jnp.float32)
        keep_squares(even_square, 1)
        each_column(relay_odd)
        odd_rows = band[pl.ds(pl.multiple_of(step * FULL + EVENS, BLOCK), ODDS), window]
        odd_square = lax.dot_general(odd_rows, shifted[...], across, preferred_element_type=jnp.float32)
        keep_squares(odd_square, 0)
        even_cube = jnp.dot(even_rows, low[BLOCK:BLOCK + WIDTH, :], preferred_element_type=jnp.float32)
        odd_cube = jnp.dot(odd_rows, low[0:WIDTH, :], preferred_element_type=jnp.float32)
        for slot in range(SLOTS):
            order = (slot - 1) // 2 if slot % 2 else slot // 2
            source = even_cube if slot % 2 else odd_cube
            kept = pat_ref[0, slot].astype(jnp.float32)
            part = squares[(1 + slot) * BLOCK:(2 + slot) * BLOCK, :]
            cube = source[order * BLOCK:(order + 1) * BLOCK, :]
            squares[(1 + slot) * BLOCK:(2 + slot) * BLOCK, :] = (3.0 * part - 2.0 * cube) * kept

        @pl.when(step < STEPS - 1)
        def _():
            for tile in range(TILES):
                part = squares[(1 + 2 * tile) * BLOCK:(3 + 2 * tile) * BLOCK, :]
                band[rows_of(step + 1, 0), (MARGIN + tile) * LANES:(MARGIN + 1 + tile) * LANES] = part.T.astype(
                    jnp.bfloat16
                )

        return 0

    lax.fori_loop(0, STEPS, purify, 0)

    for tile in range(TILES):
        part = squares[(1 + 2 * tile) * BLOCK:(3 + 2 * tile) * BLOCK, :].T
        wide = min(LANES, FULL - tile * LANES)
        out_ref[:, tile * LANES:tile * LANES + wide] = part[:, :wide]

    def finish(step, _):
        def rest(column):
            turns = len(ROUTES[column])
            for number in sent_before(column, turns - DELAY, turns):
                drain(step, column, number)

        each_column(rest)
        return 0

    lax.fori_loop(0, STEPS, finish, 0)


def solution(mesh):
    columns = mesh.shape["col"]
    lines = mesh.shape["row"] * columns // LINE

    def local(density, pattern):
        return pl.pallas_call(
            functools.partial(kernel, lines, columns),
            out_shape=jax.ShapeDtypeStruct((BLOCK, FULL), jnp.float32),
            in_specs=[
                pl.BlockSpec(memory_space=pltpu.HBM),
                pl.BlockSpec(memory_space=pltpu.HBM),
            ],
            out_specs=pl.BlockSpec(memory_space=pltpu.VMEM),
            scratch_shapes=[
                pltpu.VMEM((BLOCK, FULL), jnp.float32),
                pltpu.SMEM((1, SLOTS), jnp.int32),
                pltpu.VMEM((STEPS * FULL, STORED * LANES), jnp.bfloat16),
                pltpu.VMEM((BLOCK, WIDTH), jnp.bfloat16),
                pltpu.VMEM(((SLOTS + 2) * BLOCK, BLOCK), jnp.float32),
                pltpu.VMEM(((SLOTS + 2) * BLOCK, BLOCK), jnp.bfloat16),
                pltpu.SemaphoreType.DMA((2,)),
                pltpu.SemaphoreType.DMA((STEPS, MOST_SENDS)),
                pltpu.SemaphoreType.DMA((STEPS, len(PARTS) * SLOTS)),
            ],
            compiler_params=pltpu.CompilerParams(
                collective_id=0, has_side_effects=True, vmem_limit_bytes=40 << 20
            ),
        )(density, pattern)

    placed = (P(("row", "col"), None), P(("row", "col"), None))
    return jax.shard_map(
        local, mesh=mesh, in_specs=placed, out_specs=P(("row", "col"), None), check_vma=False
    )
```

```python
import functools

import jax
import jax.numpy as jnp
from jax import lax
from jax.experimental import pallas as pl
from jax.experimental.pallas import tpu as pltpu
from jax.sharding import PartitionSpec as P

STEPS = 2
BLOCK = 64
HALF = 9
SLOTS = 2 * HALF + 1
LANES = 128
TILES = 10
WIDTH = TILES * LANES
FULL = SLOTS * BLOCK
LINE = 8
EVENS = 9 * BLOCK
ODDS = 10 * BLOCK
MARGIN = 4
STORED = TILES + 9
PARTS = ((0, 1), (2, 3), (4, 5), (6, 7), (8, 9))
DELAY = 20
MESH = pl.DeviceIdType.MESH

ROUTES = (
    ((1, 3, 0, 1), (7, 0, 0, 7), (8, 0, 1, 0), (1, 0, 0, 1), (7, 1, 0, 7), (8, 1, 1, 0), (1, 1, 0, 1),
     (7, 2, 0, 7), (-8, 3, -1, 0), (8, 2, 1, 0), (1, 2, 0, 1), (-8, 2, -1, 0), (1, 4, 0, 1), (-8, 4, -1, 0),
     (-1, 4, 0, 7), (2, 1, 0, 1), (-7, 3, -1, 0), (6, 1, 0, 7), (9, 0, 1, 0), (2, 2, 0, 1), (-1, 0, -1, 0),
     (6, 0, 0, 7), (9, 1, 1, 0), (2, 3, 0, 1), (-1, 1, -1, 0), (-1, 3, 0, 7), (-7, 1, -1, 0), (9, 2, 1, 0),
     (2, 4, 0, 1), (6, 2, 0, 7), (-7, 2, -1, 0), (2, 0, 0, 1), (-1, 2, 0, 7), (-7, 4, -1, 0), (3, 1, 0, 1),
     (6, 3, 0, 7), (-9, 4, -1, 0), (5, 2, 0, 7), (-6, 1, -1, 0), (-6, 2, 0, 1), (5, 3, 0, 7), (-2, 1, -1, 0),
     (-2, 0, -1, 0), (-2, 2, 0, 7), (3, 0, 0, 1), (-6, 3, -1, 0), (5, 0, 0, 7), (4, 1, 0, 1), (-9, 3, -1, 0),
     (5, 1, 0, 7), (-5, 1, 0, 1), (-6, 4, -1, 0), (-2, 3, 0, 7), (4, 2, 0, 1), (-9, 2, -1, 0), (-2, 4, 0, 7),
     (-5, 3, 0, 1), (-3, 2, -1, 0), (4, 3, 0, 7), (-5, 2, 0, 1), (-3, 3, -1, 0), (4, 0, 0, 7), (-3, 0, -1, 0),
     (3, 2, 0, 7), (-4, 1, -1, 0), (-4, 4, 0, 2), (-5, 4, 0, 1), (3, 3, 0, 7), (-3, 1, -1, 0), (-3, 4, 0, 2),
     (-4, 2, 0, 1), (-4, 3, -1, 0)),
    ((-1, 2, 0, 0), (1, 1, 0, 2), (-1, 0, 0, 0), (1, 2, 0, 2), (-1, 1, 0, 0), (1, 3, 0, 2), (-8, 2, -1, 1),
     (8, 0, 1, 1), (-1, 3, 0, 0), (1, 4, 0, 2), (-8, 3, -1, 1), (8, 1, 1, 1), (-1, 4, 0, 0), (1, 0, 0, 2),
     (-8, 4, -1, 1), (8, 2, 1, 1), (2, 1, 0, 2), (-9, 2, -1, 1), (6, 3, 0, 7), (6, 0, 0, 0), (-7, 1, -1, 1),
     (7, 2, 1, 1), (2, 2, 0, 2), (6, 1, 0, 0), (-7, 2, -1, 1), (9, 1, 1, 1), (2, 3, 0, 2), (6, 2, 0, 0),
     (-7, 3, -1, 1), (7, 0, 1, 1), (2, 4, 0, 2), (9, 2, 1, 1), (-9, 3, 0, 0), (-7, 4, -1, 1), (2, 0, 0, 2),
     (7, 1, 1, 1), (-2, 4, 0, 0), (-9, 4, -1, 1), (3, 1, 0, 2), (9, 0, 1, 1), (5, 1, 0, 0), (-6, 1, -1, 1),
     (3, 2, 0, 2), (-2, 0, -1, 1), (5, 0, 0, 0), (-6, 3, 0, 2), (-6, 2, -1, 1), (-2, 3, 0, 0), (3, 3, 0, 2),
     (-2, 1, -1, 1), (5, 2, 0, 0), (3, 0, 0, 2), (-2, 2, -1, 1), (-6, 4, -1, 1), (4, 1, 0, 2), (4, 2, 0, 0),
     (-5, 1, -1, 1), (4, 3, 0, 0), (-5, 2, 0, 2), (-3, 1, -1, 1), (-3, 0, 0, 0), (-5, 3, -1, 1), (-3, 2, 0, 0),
     (4, 0, 0, 0), (-5, 4, 0, 2), (5, 3, 0, 2), (-4, 1, -1, 0), (-4, 2, -1, 1), (-3, 3, 0, 0), (-4, 3, -1, 1),
     (-3, 4, 0, 0), (-4, 4, 0, 2)),
    ((1, 1, 0, 3), (-1, 0, 0, 1), (1, 2, 0, 3), (-1, 1, 0, 1), (1, 3, 0, 3), (-8, 2, -1, 2), (-1, 2, 0, 1),
     (8, 0, 1, 2), (1, 4, 0, 3), (-8, 3, -1, 2), (-1, 3, 0, 1), (8, 1, 1, 2), (1, 0, 0, 3), (-8, 4, -1, 2),
     (-1, 4, 0, 1), (-7, 1, -1, 2), (8, 2, 1, 2), (2, 1, 0, 3), (-2, 2, 0, 1), (9, 1, 1, 2), (-7, 2, -1, 2),
     (2, 2, 0, 3), (-2, 0, 0, 1), (7, 0, 1, 2), (-7, 3, -1, 2), (2, 3, 0, 3), (9, 2, 1, 2), (-2, 1, 0, 1),
     (-9, 2, -1, 2), (2, 4, 0, 3), (7, 1, 1, 2), (-2, 3, 0, 1), (-7, 4, -1, 2), (2, 0, 0, 3), (7, 2, 1, 2),
     (-2, 4, 0, 1), (5, 3, 0, 1), (-9, 3, -1, 2), (9, 0, 1, 2), (3, 1, 0, 3), (5, 0, 0, 1), (-9, 4, -1, 2),
     (6, 2, 1, 2), (-6, 1, -1, 2), (3, 2, 0, 3), (5, 1, 0, 1), (6, 0, 1, 2), (-6, 2, -1, 2), (3, 3, 0, 3),
     (5, 2, 0, 1), (6, 1, 1, 2), (-6, 3, -1, 2), (3, 0, 0, 3), (6, 3, 1, 2), (-3, 4, 0, 1), (-6, 4, -1, 2),
     (4, 2, 0, 3), (4, 1, 0, 1), (-5, 1, -1, 2), (-3, 0, 0, 1), (4, 3, 0, 3), (-5, 2, -1, 2), (-5, 4, 0, 3),
     (4, 0, 0, 1), (-3, 1, -1, 2), (-3, 3, 0, 1), (-5, 3, -1, 2), (-3, 2, -1, 2), (-4, 4, 0, 3), (-4, 2, -1, 2),
     (-4, 1, -1, 2), (-4, 3, -1, 2)),
    ((1, 1, 0, 4), (-1, 0, 0, 2), (1, 2, 0, 4), (-1, 1, 0, 2), (1, 3, 0, 4), (-8, 2, -1, 3), (-1, 2, 0, 2),
     (8, 0, 1, 3), (1, 4, 0, 4), (-8, 3, -1, 3), (-1, 3, 0, 2), (8, 1, 1, 3), (1, 0, 0, 4), (-8, 4, -1, 3),
     (-1, 4, 0, 2), (-7, 1, -1, 3), (8, 2, 1, 3), (2, 4, 0, 4), (-2, 0, 0, 2), (9, 1, 1, 3), (-7, 2, -1, 3),
     (2, 1, 0, 4), (-2, 1, 0, 2), (7, 0, 1, 3), (-7, 3, -1, 3), (2, 2, 0, 4), (9, 2, 1, 3), (-2, 2, 0, 2),
     (-9, 2, -1, 3), (2, 3, 0, 4), (7, 1, 1, 3), (-2, 3, 0, 2), (-7, 4, -1, 3), (2, 0, 0, 4), (7, 2, 1, 3),
     (-2, 4, 0, 2), (-9, 3, -1, 3), (3, 2, 0, 4), (9, 0, 1, 3), (-3, 2, 0, 2), (-9, 4, -1, 3), (3, 3, 0, 4),
     (6, 0, 1, 3), (-3, 0, 0, 2), (-6, 4, -1, 3), (3, 1, 0, 4), (6, 1, 1, 3), (-6, 1, -1, 3), (-3, 1, 0, 2),
     (6, 2, 1, 3), (-6, 2, -1, 3), (-3, 3, 0, 2), (6, 3, 1, 3), (3, 0, 0, 4), (-5, 4, -1, 4), (5, 2, 1, 3),
     (-6, 3, -1, 3), (4, 0, 0, 2), (4, 1, 0, 4), (-5, 2, -1, 3), (5, 0, 0, 2), (5, 1, 1, 3), (5, 3, 1, 3),
     (4, 2, 0, 2), (-4, 1, -1, 4), (-5, 3, -1, 3), (-4, 4, 0, 2), (4, 3, 0, 4), (-3, 4, 0, 4), (-4, 2, -1, 4),
     (-5, 1, -1, 3), (-4, 3, -1, 4)),
    ((1, 4, 0, 5), (-1, 2, 0, 3), (1, 1, 0, 5), (-1, 3, 0, 3), (1, 2, 0, 5), (-8, 2, -1, 4), (-1, 0, 0, 3),
     (8, 0, 1, 4), (1, 3, 0, 5), (-8, 3, -1, 4), (-1, 1, 0, 3), (8, 1, 1, 4), (1, 0, 0, 5), (-8, 4, -1, 4),
     (-1, 4, 0, 3), (8, 2, 1, 4), (2, 2, 0, 5), (-7, 4, -1, 4), (-2, 0, 0, 3), (7, 2, 1, 4), (2, 3, 0, 5),
     (-9, 2, -1, 4), (-2, 1, 0, 3), (-7, 1, -1, 4), (9, 1, 1, 4), (2, 1, 0, 5), (9, 2, 1, 4), (-2, 2, 0, 3),
     (-9, 3, -1, 4), (2, 4, 0, 5), (7, 0, 1, 4), (-2, 3, 0, 3), (-7, 2, -1, 4), (2, 0, 0, 5), (7, 1, 1, 4),
     (-2, 4, 0, 3), (-7, 3, -1, 4), (9, 0, 1, 4), (-3, 0, 0, 3), (3, 1, 0, 5), (-9, 4, -1, 4), (6, 0, 1, 4),
     (-3, 1, 0, 3), (3, 2, 0, 5), (-6, 2, -1, 4), (6, 1, 1, 4), (-3, 2, 0, 3), (3, 3, 0, 5), (-6, 3, -1, 4),
     (-6, 1, -1, 4), (6, 2, 1, 4), (-3, 3, 0, 3), (3, 0, 0, 5), (6, 3, 1, 4), (-6, 4, -1, 4), (-3, 4, 0, 3),
     (5, 0, 1, 4), (-4, 4, 0, 5), (-5, 4, -1, 5), (-5, 1, -1, 4), (-4, 2, 0, 5), (4, 2, 1, 3), (5, 1, 1, 4),
     (-5, 2, -1, 4), (-4, 1, 0, 3), (-5, 3, -1, 4), (4, 0, 1, 3), (5, 2, 1, 4), (-4, 3, 0, 3), (5, 3, 1, 4),
     (4, 1, 1, 3), (4, 3, 1, 3)),
    ((1, 2, 0, 6), (-1, 3, 0, 4), (1, 3, 0, 6), (-1, 0, 0, 4), (1, 1, 0, 6), (-8, 2, -1, 5), (-1, 1, 0, 4),
     (8, 0, 1, 5), (1, 4, 0, 6), (-8, 3, -1, 5), (-1, 2, 0, 4), (8, 1, 1, 5), (1, 0, 0, 6), (-8, 4, -1, 5),
     (-1, 4, 0, 4), (8, 2, 1, 5), (-7, 2, -1, 5), (9, 2, 1, 5), (-2, 2, 0, 4), (2, 1, 0, 6), (-9, 3, -1, 5),
     (7, 0, 1, 5), (-2, 3, 0, 4), (2, 2, 0, 6), (-7, 3, -1, 5), (9, 1, 1, 5), (-2, 0, 0, 4), (2, 3, 0, 6),
     (-7, 1, -1, 5), (7, 1, 1, 5), (-2, 1, 0, 4), (2, 0, 0, 6), (-7, 4, -1, 5), (7, 2, 1, 5), (-2, 4, 0, 4),
     (2, 4, 0, 6), (-9, 2, -1, 5), (9, 0, 1, 5), (-3, 0, 0, 4), (-5, 4, 0, 6), (-9, 4, -1, 5), (-6, 1, -1, 5),
     (6, 2, 1, 5), (-3, 1, 0, 4), (-5, 2, 0, 6), (6, 3, 1, 5), (-6, 2, -1, 5), (-3, 2, 0, 4), (-5, 3, 0, 6),
     (6, 0, 1, 5), (-6, 3, -1, 5), (-3, 3, 0, 4), (6, 1, 1, 5), (-3, 4, 0, 4), (-6, 4, -1, 5), (-5, 1, 0, 6),
     (5, 0, 1, 5), (-4, 3, 0, 6), (-4, 1, 0, 4), (5, 1, 1, 5), (3, 0, 0, 6), (-4, 2, 0, 4), (5, 2, 1, 5),
     (3, 1, 0, 6), (3, 3, 1, 5), (5, 3, 1, 5), (-4, 4, 0, 6), (4, 0, 0, 4), (4, 3, 1, 5), (4, 1, 1, 5),
     (3, 2, 0, 4), (4, 2, 1, 5)),
    ((-1, 2, 0, 5), (1, 1, 0, 7), (-1, 3, 0, 5), (1, 2, 0, 7), (-8, 2, -1, 6), (-1, 0, 0, 5), (8, 0, 1, 6),
     (1, 3, 0, 7), (-8, 3, -1, 6), (-1, 1, 0, 5), (8, 1, 1, 6), (1, 0, 0, 7), (-8, 4, -1, 6), (-1, 4, 0, 5),
     (8, 2, 1, 6), (1, 4, 0, 7), (-9, 2, -1, 6), (-2, 3, 0, 5), (-7, 1, -1, 6), (7, 2, 1, 6), (-6, 4, 0, 7),
     (-2, 0, 0, 5), (9, 2, 1, 6), (-9, 3, -1, 6), (-6, 2, 0, 7), (7, 0, 1, 6), (-2, 1, 0, 5), (-7, 2, -1, 6),
     (-6, 3, 0, 7), (7, 1, 1, 6), (-2, 2, 0, 5), (-7, 3, -1, 6), (9, 1, 0, 7), (9, 0, 1, 6), (-2, 4, 0, 5),
     (-9, 4, -1, 6), (-6, 1, 0, 7), (6, 3, 1, 6), (2, 4, 1, 6), (-3, 2, 0, 5), (-7, 4, -1, 6), (-5, 3, 0, 7),
     (6, 0, 1, 6), (-3, 3, 0, 5), (2, 0, 0, 7), (2, 2, 1, 6), (-3, 0, 0, 5), (2, 1, 0, 7), (2, 3, 1, 6),
     (6, 1, 0, 5), (-5, 2, 0, 7), (6, 2, 1, 6), (-3, 1, 0, 5), (-5, 4, 0, 7), (-3, 4, 0, 5), (3, 3, 1, 6),
     (-4, 1, 0, 7), (5, 3, 1, 6), (5, 2, 0, 5), (3, 0, 0, 7), (5, 0, 1, 6), (-4, 2, 0, 7), (-4, 3, 0, 5),
     (3, 1, 0, 7), (5, 1, 1, 6), (4, 0, 0, 5), (3, 2, 0, 7), (4, 3, 1, 7), (4, 1, 1, 6), (-5, 1, 0, 5),
     (-4, 4, 0, 7), (4, 2, 1, 6)),
    ((-8, 4, -1, 7), (-7, 4, 0, 0), (-1, 1, 0, 6), (-1, 0, 0, 6), (-8, 3, -1, 7), (-7, 2, 0, 0), (-1, 2, 0, 6),
     (-8, 2, -1, 7), (-7, 3, 0, 0), (8, 1, 1, 7), (-1, 3, 0, 6), (-7, 1, 0, 0), (8, 0, 1, 7), (-1, 4, 0, 6),
     (8, 2, 1, 7), (-6, 3, 0, 0), (1, 4, 1, 7), (-2, 2, 0, 6), (1, 0, 0, 0), (7, 1, 1, 7), (-2, 3, 0, 6),
     (1, 1, 0, 0), (7, 0, 1, 7), (-9, 2, -1, 7), (-6, 1, 0, 0), (-2, 0, 0, 6), (7, 2, 1, 7), (1, 2, 0, 0),
     (-2, 1, 0, 6), (-9, 3, -1, 7), (1, 3, 1, 7), (-6, 2, 0, 0), (-2, 4, 0, 6), (-9, 4, -1, 7), (2, 3, 1, 7),
     (-6, 4, 0, 0), (-3, 3, 0, 6), (6, 2, 1, 7), (-5, 1, 0, 0), (-3, 0, 0, 6), (9, 0, 1, 7), (2, 0, 0, 0),
     (6, 3, 1, 7), (-5, 2, 0, 0), (9, 1, 1, 7), (-3, 4, 0, 6), (2, 1, 0, 0), (6, 0, 1, 7), (5, 3, 0, 6),
     (9, 2, 1, 7), (-5, 3, 0, 0), (-4, 2, 0, 6), (6, 1, 1, 7), (2, 2, 0, 0), (2, 4, 1, 7), (-4, 3, 0, 6),
     (-5, 4, 0, 0), (3, 1, 1, 7), (-4, 1, 0, 0), (4, 0, 0, 5), (5, 0, 1, 7), (5, 1, 0, 6), (-3, 1, 0, 0),
     (3, 2, 1, 7), (5, 2, 0, 6), (3, 3, 1, 7), (-3, 2, 0, 0), (3, 0, 0, 5), (4, 3, 1, 7), (-4, 4, 0, 6),
     (4, 2, 0, 6), (4, 1, 1, 7)),
)


def offset_of(d):
    return (d + 1) // 2


def line_of(y, d):
    return (y + d) // LINE


def needed_tiles(d, part):
    first, last = (0, (2 * HALF - d) // 2) if d > 0 else ((-d) // 2, TILES - 1)
    return max(first, PARTS[part][0]), min(last, PARTS[part][1])


def source_slot(y, d, line, column):
    return d + y - line * LINE - column


def receivers(column, slot, part):
    found = []
    for y in range(LINE):
        for d, piece, line, relay in ROUTES[y]:
            if relay == column and piece == part and source_slot(y, d, line, relay) == slot:
                found.append((y, d, -line))
    return found


@functools.cache
def sent_tiles(y, d, part):
    first, last = needed_tiles(d, part)
    for y_next, d_next, _ in receivers(y, d, part):
        first_next, last_next = sent_tiles(y_next, d_next, part)
        first, last = min(first, first_next), max(last, last_next)
    return first, last


@functools.cache
def depth_of(y, d, part):
    return 1 + max([depth_of(y_next, d_next, part) for y_next, d_next, _ in receivers(y, d, part)], default=0)


@functools.cache
def sends_from(column):
    own = [(0, part, *entry) for part in range(len(PARTS)) for entry in receivers(column, 0, part)]
    own.sort(key=lambda entry: -depth_of(entry[2], entry[3], entry[1]))
    relayed = [
        (d, part, *entry) for d, part, _, _ in ROUTES[column] for entry in receivers(column, d, part)
    ]
    return own + relayed


def turn_of(column, slot, part):
    return max([0] + [turn for turn, entry in enumerate(ROUTES[column]) if entry[:2] == (slot, part)])


def sent_before(column, first, last):
    return [
        number
        for number, entry in enumerate(sends_from(column))
        if first <= turn_of(column, entry[0], entry[1]) < last
    ]


def even_turns(column):
    return 1 + max(turn for turn, entry in enumerate(ROUTES[column]) if entry[0] % 2 == 0)


MOST_SENDS = max(len(sends_from(column)) for column in range(LINE))


def partners_of(column):
    found = {(line, relay) for _, _, line, relay in ROUTES[column]}
    return sorted(found | {(line, y) for _, _, y, _, line in sends_from(column)})


def kernel(lines, columns, dens_ref, pat_ref, out_ref, band, shifted, squares, low, send_sem, recv_sem):
    me = lax.axis_index("row") * columns + lax.axis_index("col")
    my_line = me // LINE
    my_column = lax.rem(me, LINE)

    def place(line, y):
        index = (my_line + line) * LINE + y
        return (index // columns, lax.rem(index, columns))

    there = {line: (my_line + line >= 0) & (my_line + line < lines) for line in range(-2, 3)}

    def rows_of(step, d):
        order = (d + HALF - 1) // 2 if d % 2 == 0 else HALF + (d + HALF) // 2
        return pl.ds(pl.multiple_of(step * FULL + order * BLOCK, BLOCK), BLOCK)

    def lanes_of(d, first, last):
        return pl.ds((MARGIN + offset_of(d) + first) * LANES, (last - first + 1) * LANES)

    def copy(step, number, slot, part, y, d, line):
        first, last = sent_tiles(y, d, part)
        return pltpu.make_async_remote_copy(
            src_ref=band.at[rows_of(step, slot), lanes_of(slot, first, last)],
            dst_ref=band.at[rows_of(step, d), lanes_of(d, first, last)],
            send_sem=send_sem.at[step, number],
            recv_sem=recv_sem.at[step, len(PARTS) * (d + HALF) + part],
            device_id=place(line, y),
            device_id_type=MESH,
        )

    def arrival(step, y, d, part):
        first, last = sent_tiles(y, d, part)
        piece = band.at[rows_of(step, d), lanes_of(d, first, last)]
        return pltpu.make_async_remote_copy(
            src_ref=piece,
            dst_ref=piece,
            send_sem=send_sem.at[step, 0],
            recv_sem=recv_sem.at[step, len(PARTS) * (d + HALF) + part],
            device_id=place(0, y),
            device_id_type=MESH,
        )

    def each_column(body):
        for column in range(LINE):
            pl.when(my_column == column)(functools.partial(body, column))

    def sent_when(column, slot, line):
        return there[line] & there[line_of(column, slot)]

    barrier = pltpu.get_barrier_semaphore()

    def greet(column):
        for line, y in partners_of(column):
            @pl.when(there[line])
            def _():
                pl.semaphore_signal(barrier, inc=1, device_id=place(line, y), device_id_type=MESH)

    def meet(column):
        count = jnp.int32(0)
        for line, _ in partners_of(column):
            count += there[line].astype(jnp.int32)
        pl.semaphore_wait(barrier, count)

    each_column(greet)
    padded = jnp.concatenate([dens_ref[...], jnp.zeros((BLOCK, WIDTH - FULL), jnp.float32)], axis=1)
    band[rows_of(0, 0), MARGIN * LANES:(MARGIN + TILES) * LANES] = padded.astype(jnp.bfloat16)
    each_column(meet)

    def clear():
        for step in range(STEPS):
            for d in range(-HALF, HALF + 1):
                off = offset_of(d)
                if d > 0:
                    band[rows_of(step, d), MARGIN * LANES:(MARGIN + off) * LANES] = jnp.zeros(
                        (BLOCK, off * LANES), jnp.bfloat16
                    )
                elif off < 0:
                    band[rows_of(step, d), (MARGIN + TILES + off) * LANES:(MARGIN + TILES) * LANES] = jnp.zeros(
                        (BLOCK, -off * LANES), jnp.bfloat16
                    )
                if d != 0:
                    @pl.when((me + d < 0) | (me + d >= lines * LINE))
                    def _():
                        band[rows_of(step, d), MARGIN * LANES:(MARGIN + TILES) * LANES] = jnp.zeros(
                            (BLOCK, WIDTH), jnp.bfloat16
                        )
        low[0:BLOCK, :] = jnp.zeros((BLOCK, BLOCK), jnp.bfloat16)
        low[(SLOTS + 1) * BLOCK:(SLOTS + 2) * BLOCK, :] = jnp.zeros((BLOCK, BLOCK), jnp.bfloat16)
        squares[(SLOTS + 1) * BLOCK:(SLOTS + 2) * BLOCK, :] = jnp.zeros((BLOCK, BLOCK), jnp.float32)
        squares[0:BLOCK, :] = jnp.zeros((BLOCK, BLOCK), jnp.float32)

    window = pl.ds(MARGIN * LANES, WIDTH)

    def keep_squares(product, odd):
        for order, slot in enumerate(range(odd, SLOTS, 2)):
            kept = pat_ref[0, slot].astype(jnp.float32)
            part = product[order * BLOCK:(order + 1) * BLOCK, :] * kept
            squares[(1 + slot) * BLOCK:(2 + slot) * BLOCK, :] = part
            low[(1 + slot) * BLOCK:(2 + slot) * BLOCK, :] = part.astype(jnp.bfloat16)

    def drain(step, column, number):
        entry = sends_from(column)[number]

        @pl.when(sent_when(column, entry[0], entry[4]))
        def _():
            copy(step, number, *entry).wait_send()

    def purify(step, _):
        def offer(column):
            for number, entry in enumerate(sends_from(column)):
                if entry[0] == 0:
                    @pl.when(sent_when(column, entry[0], entry[4]))
                    def _():
                        copy(step, number, *entry).start()

        def relay(column, first, last):
            sends = sends_from(column)
            for turn, (d, part, _, _) in enumerate(ROUTES[column]):
                if not first <= turn < last:
                    continue

                @pl.when(there[line_of(column, d)])
                def _():
                    arrival(step, column, d, part).wait_recv()

                for number, entry in enumerate(sends):
                    if entry[:2] == (d, part):
                        @pl.when(sent_when(column, d, entry[4]))
                        def _():
                            copy(step, number, *entry).start()

                for number in sent_before(column, turn - DELAY, turn - DELAY + 1):
                    drain(step, column, number)

        def relay_even(column):
            relay(column, 0, even_turns(column))

        def relay_odd(column):
            relay(column, even_turns(column), len(ROUTES[column]))

        each_column(offer)

        @pl.when(step == 0)
        def _():
            clear()
            padded = jnp.concatenate([jnp.zeros((BLOCK, BLOCK), jnp.float32), dens_ref[...]], axis=1)
            shifted[...] = padded.astype(jnp.bfloat16)

        @pl.when(step > 0)
        def _():
            for tile in range(TILES):
                part = squares[2 * tile * BLOCK:(2 + 2 * tile) * BLOCK, :]
                shifted[:, tile * LANES:(1 + tile) * LANES] = part.T.astype(jnp.bfloat16)

        each_column(relay_even)
        own = band[rows_of(step, 0), window]
        even_rows = band[pl.ds(pl.multiple_of(step * FULL, BLOCK), EVENS), window]
        across = (((1,), (1,)), ((), ()))
        even_square = lax.dot_general(even_rows, own, across, preferred_element_type=jnp.float32)
        keep_squares(even_square, 1)
        each_column(relay_odd)
        odd_rows = band[pl.ds(pl.multiple_of(step * FULL + EVENS, BLOCK), ODDS), window]
        odd_square = lax.dot_general(odd_rows, shifted[...], across, preferred_element_type=jnp.float32)
        keep_squares(odd_square, 0)
        even_cube = jnp.dot(even_rows, low[BLOCK:BLOCK + WIDTH, :], preferred_element_type=jnp.float32)
        odd_cube = jnp.dot(odd_rows, low[0:WIDTH, :], preferred_element_type=jnp.float32)
        for slot in range(SLOTS):
            order = (slot - 1) // 2 if slot % 2 else slot // 2
            source = even_cube if slot % 2 else odd_cube
            kept = pat_ref[0, slot].astype(jnp.float32)
            part = squares[(1 + slot) * BLOCK:(2 + slot) * BLOCK, :]
            cube = source[order * BLOCK:(order + 1) * BLOCK, :]
            squares[(1 + slot) * BLOCK:(2 + slot) * BLOCK, :] = (3.0 * part - 2.0 * cube) * kept

        @pl.when(step < STEPS - 1)
        def _():
            for tile in range(TILES):
                part = squares[(1 + 2 * tile) * BLOCK:(3 + 2 * tile) * BLOCK, :]
                band[rows_of(step + 1, 0), (MARGIN + tile) * LANES:(MARGIN + 1 + tile) * LANES] = part.T.astype(
                    jnp.bfloat16
                )

        return 0

    lax.fori_loop(0, STEPS, purify, 0)

    for tile in range(TILES):
        part = squares[(1 + 2 * tile) * BLOCK:(3 + 2 * tile) * BLOCK, :].T
        wide = min(LANES, FULL - tile * LANES)
        out_ref[:, tile * LANES:tile * LANES + wide] = part[:, :wide]

    def finish(step, _):
        def rest(column):
            turns = len(ROUTES[column])
            for number in sent_before(column, turns - DELAY, turns):
                drain(step, column, number)

        each_column(rest)
        return 0

    lax.fori_loop(0, STEPS, finish, 0)


def solution(mesh):
    columns = mesh.shape["col"]
    lines = mesh.shape["row"] * columns // LINE

    def local(density, pattern):
        return pl.pallas_call(
            functools.partial(kernel, lines, columns),
            out_shape=jax.ShapeDtypeStruct((BLOCK, FULL), jnp.float32),
            in_specs=[
                pl.BlockSpec(memory_space=pltpu.VMEM),
                pl.BlockSpec(memory_space=pltpu.SMEM),
            ],
            out_specs=pl.BlockSpec(memory_space=pltpu.VMEM),
            scratch_shapes=[
                pltpu.VMEM((STEPS * FULL, STORED * LANES), jnp.bfloat16),
                pltpu.VMEM((BLOCK, WIDTH), jnp.bfloat16),
                pltpu.VMEM(((SLOTS + 2) * BLOCK, BLOCK), jnp.float32),
                pltpu.VMEM(((SLOTS + 2) * BLOCK, BLOCK), jnp.bfloat16),
                pltpu.SemaphoreType.DMA((STEPS, MOST_SENDS)),
                pltpu.SemaphoreType.DMA((STEPS, len(PARTS) * SLOTS)),
            ],
            compiler_params=pltpu.CompilerParams(
                collective_id=0, has_side_effects=True, vmem_limit_bytes=40 << 20
            ),
        )(density, pattern)

    placed = (P(("row", "col"), None), P(("row", "col"), None))
    return jax.shard_map(
        local, mesh=mesh, in_specs=placed, out_specs=P(("row", "col"), None), check_vma=False
    )
```
